128 devices in a mesh: tm: 8 (over x, core), space: 16 (over y, z).
Axes of the slice: x: 4, y: 4, z: 4, core: 2. Of those that a mesh axis runs over, the one named last changes fastest.
Arguments:
- adjoint_field: float32 [1024, 48, 9216], P('tm', 'space'), may hold values from -6 to 6
- absorption: float32 [48, 9216], P('space'), may hold values from 0.25 to 2
- mode_rates: float32 [16], replicated, may hold values from 0.1 to 40
- mode_weights: float32 [16], replicated, may hold values from 0.1 to 0.5
Outputs:
- adjoint_image: float32 [1024, 48, 9216], P('tm', 'space')
The draws below stay inside these ranges and needn't reach their ends.
All inputs are finite; a program needn't handle non-finite values.
Results may differ from the reference program's by a relative error of at most 0.0001.
Values sent between devices are 32-bit elements; how exact they have to be, the bound alone decides.
A program may use at most 192 MiB of HBM per device.

```python
import math
import jax
import jax.numpy as jnp
from jax import lax

NY = 96
BAND = 16
MODES = 16
NZ = 48
TIME = 1024
PLANE = 9216


def levels(key, shape, pieces, low, high):
    loudness = 1.0
    for axis_at, shards_of in pieces:
        steps = jax.random.uniform(jax.random.fold_in(jax.random.fold_in(key, 6), axis_at), (shards_of,), jnp.float32, low / len(pieces), high / len(pieces))
        loudness = loudness * jnp.repeat(jnp.exp(steps), shape[axis_at] // shards_of).reshape((-1,) + (1,) * (len(shape) - 1 - axis_at))
    return loudness


def normal_values(rng, shape, deviation, limit, cuts=(), kind=jnp.bfloat16):
    gain = levels(rng, shape, cuts, -0.22, 0.18) if cuts else 1.0
    entries = jax.random.normal(rng, shape, jnp.float32) * deviation * gain
    return jnp.minimum(jnp.maximum(entries, -limit), limit).astype(kind)


def setup_inputs(seed: int = 0) -> dict:
    arg_keys = jax.random.split(jax.random.key(seed), 5)
    adjoint_field = normal_values(arg_keys[0], (TIME, NZ, PLANE), 1.0, 6.0, ((0, 8), (1, 16)), jnp.float32)
    absorption = jnp.clip(0.25 + 1.75 * jax.random.uniform(arg_keys[1], (NZ, PLANE), jnp.float32) ** levels(arg_keys[1], (NZ, PLANE), ((0, 16),), -0.2, 0.2), 0.25, 2.0)
    mode_rates = jnp.clip(jnp.exp(jax.random.uniform(arg_keys[2], (MODES,), jnp.float32, math.log(0.1), math.log(40.0))), 0.1, 40.0)
    mode_weights = jnp.clip(jnp.exp(jax.random.uniform(arg_keys[3], (MODES,), jnp.float32, math.log(0.1), math.log(0.5))), 0.1, 0.5)
    return {"adjoint_field": adjoint_field, "absorption": absorption, "mode_rates": mode_rates, "mode_weights": mode_weights}


DIFFUSION = 0.2
ORDER_EXP = 0.4
STENCIL = (-1.0 / 12.0, 16.0 / 12.0, -30.0 / 12.0, 16.0 / 12.0, -1.0 / 12.0)

def caputo_weights(count):
    steps_idx = jnp.arange(count, dtype=jnp.float32)
    increments = (steps_idx + 1.0) ** ORDER_EXP - steps_idx ** ORDER_EXP
    earlier = jnp.concatenate([jnp.zeros((1,), jnp.float32), increments[:-1]])
    return increments - earlier

def mode_tables(mode_rates, mode_weights, total_steps):
    scaled = mode_rates / total_steps
    decays = jnp.exp(-scaled)
    mode_gain = mode_weights * jnp.sqrt(-jnp.expm1(-2.0 * scaled))
    return (scaled, decays, mode_gain)

def band_weights(scaled, mode_gain):
    offsets = jnp.arange(BAND, dtype=jnp.float32)
    far_part = lax.optimization_barrier(jnp.sum(mode_gain[:, None] * jnp.exp(-scaled[:, None] * offsets[None, :]), axis=0))
    return caputo_weights(BAND) - far_part

def plane_masks(row_len, plane_len):
    column = jnp.arange(plane_len, dtype=jnp.int32) % row_len
    return [((column + offset >= 0) & (column + offset < row_len)).astype(jnp.float32) for offset in (-2, -1, 1, 2)]

def laplacian(padded, slab_depth, row_len):
    plane_len = padded.shape[-1]
    center = padded[..., 2:2 + slab_depth, :]
    summed = 3.0 * STENCIL[2] * center
    for offset in (-2, -1, 1, 2):
        summed = summed + STENCIL[offset + 2] * padded[..., 2 + offset:2 + offset + slab_depth, :]
    widths = [(0, 0)] * (center.ndim - 1) + [(2 * row_len, 2 * row_len)]
    spread = jnp.pad(center, widths)
    y_masks = plane_masks(row_len, plane_len)
    for position, offset in enumerate((-2, -1, 1, 2)):
        weight = STENCIL[offset + 2]
        anchor = 2 * row_len + offset * row_len
        summed = summed + weight * spread[..., anchor:anchor + plane_len]
        anchor = 2 * row_len + offset
        summed = summed + weight * y_masks[position] * spread[..., anchor:anchor + plane_len]
    return summed

def reference(adjoint_field, absorption, mode_rates, mode_weights):
    scaled, decays, mode_gain = mode_tables(mode_rates, mode_weights, TIME)
    weights = band_weights(scaled, mode_gain)

    def advance(state_pair, current):
        mode_sums, window = state_pair
        mode_sums = current[None] + decays[:, None, None] * mode_sums
        stacked = jnp.concatenate([current[None], window], axis=0)
        history = jnp.tensordot(weights, stacked, axes=1, precision=lax.Precision.HIGHEST)
        history = history + jnp.tensordot(mode_gain, mode_sums, axes=1, precision=lax.Precision.HIGHEST)
        padded = jnp.pad(current, ((2, 2), (0, 0)))
        outcome = history + absorption * current - DIFFUSION * laplacian(padded, NZ, NY)
        return ((mode_sums, stacked[:-1]), outcome)
    initial = (jnp.zeros((MODES, NZ, PLANE), jnp.float32), jnp.zeros((BAND - 1, NZ, PLANE), jnp.float32))
    final_state, images = lax.scan(advance, initial, adjoint_field, reverse=True)
    return images
```

```python
import jax
import jax.numpy as jnp
from jax import lax
from jax.experimental import pallas as pl
from jax.experimental.pallas import tpu as pltpu
from jax.sharding import PartitionSpec as P


NY = 96
BAND = 16
DIFFUSION = 0.2
ORDER_EXP = 0.4
EDGE = 256
TILE = 2304
CHUNKS = (16, 64, 40, 8)
EXACT = lax.Precision.HIGHEST


def caputo_weights(count):
    steps_idx = jnp.arange(count, dtype=jnp.float32)
    increments = (steps_idx + 1.0) ** ORDER_EXP - steps_idx**ORDER_EXP
    earlier = jnp.concatenate([jnp.zeros((1,), jnp.float32), increments[:-1]])
    return increments - earlier


def history_tables(scaled, mode_gain, steps_dev):
    span_len = steps_dev + BAND
    row_idx = jnp.arange(steps_dev, dtype=jnp.int32)[:, None]
    col_idx = jnp.arange(span_len, dtype=jnp.int32)[None, :]
    lag = col_idx - row_idx
    lag_clip = jnp.clip(lag, 0, span_len).astype(jnp.float32)
    far = jnp.sum(
        mode_gain[:, None, None] * jnp.exp(-scaled[:, None, None] * lag_clip[None]), axis=0
    )
    onehot = (lag[None] == jnp.arange(BAND, dtype=jnp.int32)[:, None, None]).astype(jnp.float32)
    near = jnp.sum(caputo_weights(BAND)[:, None, None] * onehot, axis=0)
    in_band = (lag >= 0) & (lag < BAND)
    own = near + jnp.where(lag >= BAND, far, 0.0)
    ahead = jnp.where(in_band, near - far, 0.0)
    step_pos = jnp.arange(steps_dev, dtype=jnp.float32)
    remote = mode_gain[None, :] * jnp.exp(-scaled[None, :] * (steps_dev - step_pos)[:, None])
    table = jnp.concatenate(
        [jnp.where(col_idx < steps_dev, own, ahead), remote], axis=1
    )
    projector = jnp.exp(-scaled[:, None] * step_pos[None, :])
    return table, projector


def project_kernel(projector_ref, field_ref, out_ref):
    out_ref[0] = jnp.dot(
        projector_ref[...], field_ref[0], precision=EXACT, preferred_element_type=jnp.float32
    )


def block_sums(projector, field):
    depth, steps, plane = field.shape
    modes = projector.shape[0]
    return pl.pallas_call(
        project_kernel,
        out_shape=jax.ShapeDtypeStruct((depth, modes, plane), jnp.float32),
        grid=(depth, plane // TILE),
        in_specs=[
            pl.BlockSpec((modes, steps), lambda p, i: (0, 0)),
            pl.BlockSpec((1, steps, TILE), lambda p, i: (p, 0, i)),
        ],
        out_specs=pl.BlockSpec((1, modes, TILE), lambda p, i: (p, 0, i)),
        cost_estimate=pl.CostEstimate(
            flops=12 * modes * steps * depth * plane,
            bytes_accessed=4 * depth * plane * (steps + modes),
            transcendentals=0,
        ),
        name="block_sums",
    )(projector, field)


def local_kernel(
    table_ref, left_ref, mid_ref, right_ref, head_ref, carried_ref, absorb_ref, out_ref, wide, masks
):
    depth, steps, width = mid_ref.shape
    spot, spots = pl.program_id(0), pl.num_programs(0)
    column = lax.broadcasted_iota(jnp.int32, (8, width), 1) % NY
    for k, offset in enumerate((-2, -1, 1, 2)):
        good = (column + offset >= 0) & (column + offset < NY)
        masks[k] = jnp.where(good, 16.0 if offset in (-1, 1) else -1.0, 0.0)
    has_left = jnp.where(spot > 0, 1.0, 0.0)
    has_right = jnp.where(spot < spots - 1, 1.0, 0.0)
    factor = -DIFFUSION / 12.0
    for p in range(depth):
        wide[0:steps, 0:EDGE] = left_ref[p] * has_left
        wide[0:steps, EDGE : EDGE + width] = mid_ref[p]
        wide[0:steps, EDGE + width :] = right_ref[p] * has_right
        wide[steps : steps + BAND, EDGE : EDGE + width] = head_ref[p]
        wide[steps + BAND :, EDGE : EDGE + width] = carried_ref[p]
        out_ref[p] = jnp.dot(
            table_ref[...],
            wide[:, EDGE : EDGE + width],
            precision=EXACT,
            preferred_element_type=jnp.float32,
        )
        absorb = jnp.broadcast_to(absorb_ref[pl.ds(p, 1), :], (8, width)) - 90.0 * factor

        def some_steps(t, _, p=p, absorb=absorb):
            rows = pl.ds(pl.multiple_of(t * 8, 8), 8)

            def at(offset):
                return wide[rows, EDGE + offset : EDGE + offset + width]

            center = mid_ref[p, rows, :]
            near = at(-NY) + at(NY)
            far = at(-2 * NY) + at(2 * NY)
            for q in range(depth):
                if abs(q - p) == 1:
                    near = near + mid_ref[q, rows, :]
                if abs(q - p) == 2:
                    far = far + mid_ref[q, rows, :]
            total = 16.0 * near - far
            for k, offset in enumerate((-2, -1, 1, 2)):
                total = total + masks[k] * at(offset)
            out_ref[p, rows, :] = out_ref[p, rows, :] + absorb * center + factor * total
            return 0

        lax.fori_loop(0, steps // 8, some_steps, 0)


def local_part(table, field, head, carried, absorption):
    depth, steps, plane = field.shape
    per = TILE // EDGE
    last = plane // EDGE - 1
    cols = table.shape[1]
    return pl.pallas_call(
        local_kernel,
        out_shape=jax.ShapeDtypeStruct(field.shape, jnp.float32),
        grid=(plane // TILE,),
        in_specs=[
            pl.BlockSpec((steps, cols), lambda i: (0, 0)),
            pl.BlockSpec((depth, steps, EDGE), lambda i: (0, 0, jnp.maximum(i * per - 1, 0))),
            pl.BlockSpec((depth, steps, TILE), lambda i: (0, 0, i)),
            pl.BlockSpec((depth, steps, EDGE), lambda i: (0, 0, jnp.minimum(i * per + per, last))),
            pl.BlockSpec((depth, BAND, TILE), lambda i: (0, 0, i)),
            pl.BlockSpec((depth, cols - steps - BAND, TILE), lambda i: (0, 0, i)),
            pl.BlockSpec((depth, TILE), lambda i: (0, i)),
        ],
        out_specs=pl.BlockSpec((depth, steps, TILE), lambda i: (0, 0, i)),
        scratch_shapes=[
            pltpu.VMEM((cols, TILE + 2 * EDGE), jnp.float32),
            pltpu.VMEM((4, 8, TILE), jnp.float32),
        ],
        compiler_params=pltpu.CompilerParams(vmem_limit_bytes=48 * 1024 * 1024),
        cost_estimate=pl.CostEstimate(
            flops=12 * cols * steps * depth * plane,
            bytes_accessed=8 * depth * plane * steps,
            transcendentals=0,
        ),
        name="local_part",
    )(table, field, field, field, head, carried, absorption)


def edge_kernel(image_ref, below_ref, above_ref, out_ref):
    depth = image_ref.shape[0]
    factor = -DIFFUSION / 12.0
    ends = [None] * depth

    def add(p, value):
        if 0 <= p < depth:
            ends[p] = value if ends[p] is None else ends[p] + value

    add(0, 16.0 * below_ref[1] - below_ref[0])
    add(1, -below_ref[1])
    add(depth - 1, 16.0 * above_ref[0] - above_ref[1])
    add(depth - 2, -above_ref[0])
    for p in range(depth):
        image = image_ref[p]
        out_ref[p] = image if ends[p] is None else image + factor * ends[p]


def add_edges(image, below, above, first, rows, width):
    depth, _, plane = image.shape
    count = below.shape[1]
    at = first // rows
    return pl.pallas_call(
        edge_kernel,
        out_shape=jax.ShapeDtypeStruct(image.shape, jnp.float32),
        grid=(count // rows, plane // width),
        in_specs=[
            pl.BlockSpec((depth, rows, width), lambda i, j: (0, at + i, j)),
            pl.BlockSpec((2, rows, width), lambda i, j: (0, i, j)),
            pl.BlockSpec((2, rows, width), lambda i, j: (0, i, j)),
        ],
        out_specs=pl.BlockSpec((depth, rows, width), lambda i, j: (0, at + i, j)),
        input_output_aliases={0: 0},
        cost_estimate=pl.CostEstimate(
            flops=8 * depth * count * plane,
            bytes_accessed=4 * count * plane * (2 * depth + 4),
            transcendentals=0,
        ),
        name="add_edges",
    )(image, below, above)


def per_device(adjoint_field, absorption, mode_rates, mode_weights):
    steps, depth, plane = adjoint_field.shape
    groups = lax.axis_size("tm")
    slabs = lax.axis_size("space")
    field = jnp.transpose(adjoint_field, (1, 0, 2))

    up = [(i, i + 1) for i in range(slabs - 1)]
    down = [(i + 1, i) for i in range(slabs - 1)]
    below, above, starts = [], [], []
    first = 0
    source = field
    for count in CHUNKS:
        starts.append(first)
        high = source[depth - 2 :, first : first + count]
        low = source[:2, first : first + count]
        below.append(lax.ppermute(high, "space", up))
        above.append(lax.ppermute(low, "space", down))
        source, _, _ = lax.optimization_barrier((source, high, low))
        if len(starts) == 2:
            early = source
        first += count

    scaled = mode_rates / (steps * groups)
    mode_gain = mode_weights * jnp.sqrt(-jnp.expm1(-2.0 * scaled))
    table, projector = history_tables(scaled, mode_gain, steps)

    head = lax.ppermute(early[:, :BAND], "tm", [(g + 1, g) for g in range(groups - 1)])
    sums = block_sums(projector, early)
    decay = jnp.exp(-scaled * steps)[None, :, None]
    swap = [(g, g + 1 - 2 * (g % 2)) for g in range(groups)]
    other = lax.ppermute(sums, "tm", swap)
    core = lax.axis_index("tm") % 2
    half = plane // 2
    mine_half = lax.dynamic_slice_in_dim(sums, core * half, half, axis=2)
    other_half = lax.dynamic_slice_in_dim(other, core * half, half, axis=2)
    pair_half = jnp.where(
        core == 0, mine_half + decay * other_half, other_half + decay * mine_half
    )
    later = None
    for _ in range(groups // 2 - 1):
        sent = pair_half if later is None else pair_half + decay * decay * later
        later = lax.ppermute(sent, "tm", [(g + 2, g) for g in range(groups - 2)])
    later_other = lax.ppermute(later, "tm", swap)
    later_full = jnp.where(
        core == 0,
        jnp.concatenate([later, later_other], axis=2),
        jnp.concatenate([later_other, later], axis=2),
    )
    carried = jnp.where(core == 0, other + decay * later_full, later_full)

    image = local_part(table, field, head, carried, absorption)
    for first, lower, upper in zip(starts, below, above):
        count = lower.shape[1]
        image = add_edges(image, lower, upper, first, 8, plane if count > 8 else TILE)
    return jnp.transpose(image, (1, 0, 2))


def solution(mesh):
    return jax.shard_map(
        per_device,
        mesh=mesh,
        in_specs=(P("tm", "space", None), P("space", None), P(), P()),
        out_specs=P("tm", "space", None),
        check_vma=False,
    )
```

```python
import jax
import jax.numpy as jnp
from jax import lax
from jax.experimental import pallas as pl
from jax.experimental.pallas import tpu as pltpu
from jax.sharding import PartitionSpec as P


NY = 96
BAND = 16
DIFFUSION = 0.2
ORDER_EXP = 0.4
EDGE = 256
TILE = 2304
SPAN = 768
CHUNKS = (16, 24, 56, 24, 8)


def caputo_weights(count):
    steps_idx = jnp.arange(count, dtype=jnp.float32)
    increments = (steps_idx + 1.0) ** ORDER_EXP - steps_idx**ORDER_EXP
    earlier = jnp.concatenate([jnp.zeros((1,), jnp.float32), increments[:-1]])
    return increments - earlier


def history_tables(scaled, mode_gain, steps_dev):
    span_len = steps_dev + BAND
    row_idx = jnp.arange(steps_dev, dtype=jnp.int32)[:, None]
    col_idx = jnp.arange(span_len, dtype=jnp.int32)[None, :]
    lag = col_idx - row_idx
    lag_clip = jnp.clip(lag, 0, span_len).astype(jnp.float32)
    far = jnp.sum(
        mode_gain[:, None, None] * jnp.exp(-scaled[:, None, None] * lag_clip[None]), axis=0
    )
    onehot = (lag[None] == jnp.arange(BAND, dtype=jnp.int32)[:, None, None]).astype(jnp.float32)
    near = jnp.sum(caputo_weights(BAND)[:, None, None] * onehot, axis=0)
    in_band = (lag >= 0) & (lag < BAND)
    own = near + jnp.where(lag >= BAND, far, 0.0)
    ahead = jnp.where(in_band, near - far, 0.0)
    step_pos = jnp.arange(steps_dev, dtype=jnp.float32)
    remote = mode_gain[None, :] * jnp.exp(-scaled[None, :] * (steps_dev - step_pos)[:, None])
    table = jnp.concatenate(
        [jnp.where(col_idx < steps_dev, own, ahead), remote], axis=1
    )
    projector = jnp.exp(-scaled[:, None] * step_pos[None, :])
    return table, projector


def parts(value):
    high = value.astype(jnp.bfloat16)
    return high, (value - high.astype(jnp.float32)).astype(jnp.bfloat16)


def product(weights, high, low):
    rows = weights.shape[0]
    upper, lower = parts(weights)
    both = jnp.dot(
        jnp.concatenate([upper, lower], axis=0), high, preferred_element_type=jnp.float32
    )
    rest = jnp.dot(upper, low, preferred_element_type=jnp.float32)
    return both[:rows] + both[rows:] + rest


def project_kernel(projector_ref, field_ref, out_ref):
    high, low = parts(field_ref[0])
    out_ref[0] = product(projector_ref[...], high, low)


def block_sums(projector, field):
    depth, steps, plane = field.shape
    modes = projector.shape[0]
    return pl.pallas_call(
        project_kernel,
        out_shape=jax.ShapeDtypeStruct((depth, modes, plane), jnp.float32),
        grid=(depth, plane // TILE),
        in_specs=[
            pl.BlockSpec((modes, steps), lambda p, i: (0, 0)),
            pl.BlockSpec((1, steps, TILE), lambda p, i: (p, 0, i)),
        ],
        out_specs=pl.BlockSpec((1, modes, TILE), lambda p, i: (p, 0, i)),
        cost_estimate=pl.CostEstimate(
            flops=6 * modes * steps * depth * plane,
            bytes_accessed=4 * depth * plane * (steps + modes),
            transcendentals=0,
        ),
        name="block_sums",
    )(projector, field)


def stencil_bands():
    shape = (SPAN // EDGE, SPAN, EDGE)
    lane_out = lax.broadcasted_iota(jnp.int32, shape, 2)
    offset = lax.broadcasted_iota(jnp.int32, shape, 1) - EDGE - lane_out
    column = (lax.broadcasted_iota(jnp.int32, shape, 0) * EDGE + lane_out) % NY
    inside = (column + offset >= 0) & (column + offset < NY)
    size = jnp.abs(offset)
    near = (size == NY) | ((size == 1) & inside)
    far = (size == 2 * NY) | ((size == 2) & inside)
    return jnp.where(near, 16.0, jnp.where(far, -1.0, 0.0)).astype(jnp.bfloat16)


def local_kernel(
    table_ref,
    bands_ref,
    left_ref,
    mid_ref,
    right_ref,
    head_ref,
    carried_ref,
    absorb_ref,
    out_ref,
    high_ref,
    low_ref,
):
    depth, steps, width = mid_ref.shape
    spot, spots = pl.program_id(0), pl.num_programs(0)
    has_left = jnp.where(spot > 0, 1.0, 0.0)
    has_right = jnp.where(spot < spots - 1, 1.0, 0.0)
    factor = -DIFFUSION / 12.0
    table = table_ref[...]

    def put(p, rows, lanes, value):
        high, low = parts(value)
        high_ref[p, rows, lanes] = high
        low_ref[p, rows, lanes] = low

    own, ahead, later = slice(0, steps), slice(steps, steps + BAND), slice(steps + BAND, None)
    inner = slice(EDGE, EDGE + width)
    for p in range(depth):
        put(p, own, slice(0, EDGE), left_ref[p] * has_left)
        put(p, own, inner, mid_ref[p])
        put(p, own, slice(EDGE + width, None), right_ref[p] * has_right)
        put(p, ahead, inner, head_ref[p])
        put(p, later, inner, carried_ref[p])

    def one_span(g, _):
        base = pl.multiple_of(g * SPAN, SPAN)
        span = pl.ds(base, SPAN)
        inner_span = pl.ds(pl.multiple_of(base + EDGE, EDGE), SPAN)
        for p in range(depth):
            total = product(table, high_ref[p, :, inner_span], low_ref[p, :, inner_span])
            near, far = 0.0, 0.0
            for q in range(depth):
                if abs(q - p) == 1:
                    near = near + mid_ref[q, :, span]
                if abs(q - p) == 2:
                    far = far + mid_ref[q, :, span]
            scale = absorb_ref[pl.ds(p, 1), span] - 90.0 * factor
            out_ref[p, :, span] = (
                total + scale * mid_ref[p, :, span] + factor * (16.0 * near - far)
            )
        for k in range(SPAN // EDGE):
            window = pl.ds(pl.multiple_of(base + k * EDGE, EDGE), SPAN)
            tile = pl.ds(pl.multiple_of(base + k * EDGE, EDGE), EDGE)
            high = jnp.concatenate([high_ref[p, own, window] for p in range(depth)], axis=0)
            low = jnp.concatenate([low_ref[p, own, window] for p in range(depth)], axis=0)
            around = jnp.dot(high, bands_ref[k], preferred_element_type=jnp.float32)
            around = around + jnp.dot(low, bands_ref[k], preferred_element_type=jnp.float32)
            for p in range(depth):
                out_ref[p, :, tile] += factor * around[p * steps : (p + 1) * steps]
        return 0

    lax.fori_loop(0, width // SPAN, one_span, 0)


def local_part(table, bands, field, head, carried, absorption):
    depth, steps, plane = field.shape
    per = TILE // EDGE
    last = plane // EDGE - 1
    cols = table.shape[1]
    wide = (depth, cols, TILE + 2 * EDGE)
    return pl.pallas_call(
        local_kernel,
        out_shape=jax.ShapeDtypeStruct(field.shape, jnp.float32),
        grid=(plane // TILE,),
        in_specs=[
            pl.BlockSpec((steps, cols), lambda i: (0, 0)),
            pl.BlockSpec(bands.shape, lambda i: (0, 0, 0)),
            pl.BlockSpec((depth, steps, EDGE), lambda i: (0, 0, jnp.maximum(i * per - 1, 0))),
            pl.BlockSpec((depth, steps, TILE), lambda i: (0, 0, i)),
            pl.BlockSpec((depth, steps, EDGE), lambda i: (0, 0, jnp.minimum(i * per + per, last))),
            pl.BlockSpec((depth, BAND, TILE), lambda i: (0, 0, i)),
            pl.BlockSpec((depth, cols - steps - BAND, TILE), lambda i: (0, 0, i)),
            pl.BlockSpec((depth, TILE), lambda i: (0, i)),
        ],
        out_specs=pl.BlockSpec((depth, steps, TILE), lambda i: (0, 0, i)),
        scratch_shapes=[pltpu.VMEM(wide, jnp.bfloat16), pltpu.VMEM(wide, jnp.bfloat16)],
        compiler_params=pltpu.CompilerParams(vmem_limit_bytes=48 * 1024 * 1024),
        cost_estimate=pl.CostEstimate(
            flops=6 * cols * steps * depth * plane,
            bytes_accessed=8 * depth * plane * steps,
            transcendentals=0,
        ),
        name="local_part",
    )(table, bands, field, field, field, head, carried, absorption)


def edge_kernel(image_ref, below_ref, above_ref, out_ref):
    depth = image_ref.shape[0]
    factor = -DIFFUSION / 12.0
    ends = [None] * depth

    def add(p, value):
        if 0 <= p < depth:
            ends[p] = value if ends[p] is None else ends[p] + value

    add(0, 16.0 * below_ref[1] - below_ref[0])
    add(1, -below_ref[1])
    add(depth - 1, 16.0 * above_ref[0] - above_ref[1])
    add(depth - 2, -above_ref[0])
    for p in range(depth):
        image = image_ref[p]
        out_ref[p] = image if ends[p] is None else image + factor * ends[p]


def add_edges(image, below, above, first, rows, width):
    depth, _, plane = image.shape
    count = below.shape[1]
    at = first // rows
    return pl.pallas_call(
        edge_kernel,
        out_shape=jax.ShapeDtypeStruct(image.shape, jnp.float32),
        grid=(count // rows, plane // width),
        in_specs=[
            pl.BlockSpec((depth, rows, width), lambda i, j: (0, at + i, j)),
            pl.BlockSpec((2, rows, width), lambda i, j: (0, i, j)),
            pl.BlockSpec((2, rows, width), lambda i, j: (0, i, j)),
        ],
        out_specs=pl.BlockSpec((depth, rows, width), lambda i, j: (0, at + i, j)),
        input_output_aliases={0: 0},
        cost_estimate=pl.CostEstimate(
            flops=8 * depth * count * plane,
            bytes_accessed=4 * count * plane * (2 * depth + 4),
            transcendentals=0,
        ),
        name="add_edges",
    )(image, below, above)


def per_device(adjoint_field, absorption, mode_rates, mode_weights):
    steps, depth, plane = adjoint_field.shape
    groups = lax.axis_size("tm")
    slabs = lax.axis_size("space")
    field = jnp.transpose(adjoint_field, (1, 0, 2))

    up = [(i, i + 1) for i in range(slabs - 1)]
    down = [(i + 1, i) for i in range(slabs - 1)]
    below, above, starts = [], [], []
    first = 0
    source = field
    for count in CHUNKS:
        starts.append(first)
        high = source[depth - 2 :, first : first + count]
        low = source[:2, first : first + count]
        below.append(lax.ppermute(high, "space", up))
        above.append(lax.ppermute(low, "space", down))
        source, _, _ = lax.optimization_barrier((source, high, low))
        if len(starts) == 1:
            early = source
        first += count

    scaled = mode_rates / (steps * groups)
    mode_gain = mode_weights * jnp.sqrt(-jnp.expm1(-2.0 * scaled))
    table, projector = history_tables(scaled, mode_gain, steps)

    mine_first = early[:, :BAND]
    head = lax.ppermute(mine_first, "tm", [(g + 1, g) for g in range(groups - 1)])
    sums = block_sums(projector, early)
    decay = jnp.exp(-scaled * steps)[None, :, None]
    swap = [(g, g + 1 - 2 * (g % 2)) for g in range(groups)]
    other = lax.ppermute(sums, "tm", swap)
    core = lax.axis_index("tm") % 2
    half = plane // 2
    mine_half = lax.dynamic_slice_in_dim(sums, core * half, half, axis=2)
    other_half = lax.dynamic_slice_in_dim(other, core * half, half, axis=2)
    pair_half = jnp.where(
        core == 0, mine_half + decay * other_half, other_half + decay * mine_half
    )
    later = None
    for _ in range(groups // 2 - 1):
        sent = pair_half if later is None else pair_half + decay * decay * later
        later = lax.ppermute(sent, "tm", [(g + 2, g) for g in range(groups - 2)])
    later_other = lax.ppermute(later, "tm", swap)
    later_full = jnp.where(
        core == 0,
        jnp.concatenate([later, later_other], axis=2),
        jnp.concatenate([later_other, later], axis=2),
    )
    carried = jnp.where(core == 0, other + decay * later_full, later_full)

    image = local_part(table, stencil_bands(), field, head, carried, absorption)
    for first, lower, upper in zip(starts, below, above):
        count = lower.shape[1]
        image = add_edges(image, lower, upper, first, 8, plane if count > 8 else TILE)
    return jnp.transpose(image, (1, 0, 2))


def solution(mesh):
    return jax.shard_map(
        per_device,
        mesh=mesh,
        in_specs=(P("tm", "space", None), P("space", None), P(), P()),
        out_specs=P("tm", "space", None),
        check_vma=False,
    )
```

```python
import functools

import jax
import jax.numpy as jnp
from jax import lax
from jax.experimental import pallas as pl
from jax.experimental.pallas import tpu as pltpu
from jax.sharding import PartitionSpec as P


NY = 96
BAND = 16
DIFFUSION = 0.2
ORDER_EXP = 0.4
EDGE = 256
TILE = 2304
SPAN = 768
MIB = 1024 * 1024
CHUNKS = (8, 24, 64, 24, 8)


def caputo_weights(count):
    steps_idx = jnp.arange(count, dtype=jnp.float32)
    increments = (steps_idx + 1.0) ** ORDER_EXP - steps_idx**ORDER_EXP
    earlier = jnp.concatenate([jnp.zeros((1,), jnp.float32), increments[:-1]])
    return increments - earlier


def history_tables(scaled, mode_gain, steps_dev):
    span_len = steps_dev + BAND
    row_idx = jnp.arange(steps_dev, dtype=jnp.int32)[:, None]
    col_idx = jnp.arange(span_len, dtype=jnp.int32)[None, :]
    lag = col_idx - row_idx
    lag_clip = jnp.clip(lag, 0, span_len).astype(jnp.float32)
    far = jnp.sum(
        mode_gain[:, None, None] * jnp.exp(-scaled[:, None, None] * lag_clip[None]), axis=0
    )
    onehot = (lag[None] == jnp.arange(BAND, dtype=jnp.int32)[:, None, None]).astype(jnp.float32)
    near = jnp.sum(caputo_weights(BAND)[:, None, None] * onehot, axis=0)
    in_band = (lag >= 0) & (lag < BAND)
    own = near + jnp.where(lag >= BAND, far, 0.0)
    ahead = jnp.where(in_band, near - far, 0.0)
    step_pos = jnp.arange(steps_dev, dtype=jnp.float32)
    remote = mode_gain[None, :] * jnp.exp(-scaled[None, :] * (steps_dev - step_pos)[:, None])
    table = jnp.concatenate(
        [jnp.where(col_idx < steps_dev, own, ahead), remote], axis=1
    )
    projector = jnp.exp(-scaled[:, None] * step_pos[None, :])
    return table, projector


def parts(value):
    high = value.astype(jnp.bfloat16)
    return high, (value - high.astype(jnp.float32)).astype(jnp.bfloat16)


def product(weights, high, low):
    rows = weights.shape[0]
    upper, lower = parts(weights)
    both = jnp.dot(
        jnp.concatenate([upper, lower], axis=0), high, preferred_element_type=jnp.float32
    )
    rest = jnp.dot(upper, low, preferred_element_type=jnp.float32)
    return both[:rows] + both[rows:] + rest


def project_kernel(projector_ref, field_ref, out_ref):
    high, low = parts(field_ref[0])
    out_ref[0] = product(projector_ref[...], high, low)


def block_sums(projector, field):
    depth, steps, plane = field.shape
    modes = projector.shape[0]
    return pl.pallas_call(
        project_kernel,
        out_shape=jax.ShapeDtypeStruct((depth, modes, plane), jnp.float32),
        grid=(depth, plane // TILE),
        in_specs=[
            pl.BlockSpec((modes, steps), lambda p, i: (0, 0)),
            pl.BlockSpec((1, steps, TILE), lambda p, i: (p, 0, i)),
        ],
        out_specs=pl.BlockSpec((1, modes, TILE), lambda p, i: (p, 0, i)),
        cost_estimate=pl.CostEstimate(
            flops=6 * modes * steps * depth * plane,
            bytes_accessed=4 * depth * plane * (steps + modes),
            transcendentals=0,
        ),
        compiler_params=pltpu.CompilerParams(vmem_limit_bytes=16 * MIB),
        name="block_sums",
    )(projector, field)


def stencil_bands():
    shape = (SPAN // EDGE, SPAN, EDGE)
    lane_out = lax.broadcasted_iota(jnp.int32, shape, 2)
    offset = lax.broadcasted_iota(jnp.int32, shape, 1) - EDGE - lane_out
    column = (lax.broadcasted_iota(jnp.int32, shape, 0) * EDGE + lane_out) % NY
    inside = (column + offset >= 0) & (column + offset < NY)
    size = jnp.abs(offset)
    near = (size == NY) | ((size == 1) & inside)
    far = (size == 2 * NY) | ((size == 2) & inside)
    return jnp.where(near, 16.0, jnp.where(far, -1.0, 0.0)).astype(jnp.bfloat16)


def local_kernel(
    table_ref,
    bands_ref,
    left_ref,
    mid_ref,
    right_ref,
    head_ref,
    carried_ref,
    absorb_ref,
    out_ref,
    high_ref,
    low_ref,
):
    depth, steps, width = mid_ref.shape
    spot, spots = pl.program_id(0), pl.num_programs(0)
    has_left = jnp.where(spot > 0, 1.0, 0.0)
    has_right = jnp.where(spot < spots - 1, 1.0, 0.0)
    factor = -DIFFUSION / 12.0
    table = table_ref[...]

    def put(p, rows, lanes, value):
        high, low = parts(value)
        high_ref[p, rows, lanes] = high
        low_ref[p, rows, lanes] = low

    own, ahead, later = slice(0, steps), slice(steps, steps + BAND), slice(steps + BAND, None)
    inner = slice(EDGE, EDGE + width)
    for p in range(depth):
        put(p, own, slice(0, EDGE), left_ref[p] * has_left)
        put(p, own, inner, mid_ref[p])
        put(p, own, slice(EDGE + width, None), right_ref[p] * has_right)
        put(p, ahead, inner, head_ref[p])
        put(p, later, inner, carried_ref[p])

    def one_span(g, _):
        base = pl.multiple_of(g * SPAN, SPAN)
        span = pl.ds(base, SPAN)
        inner_span = pl.ds(pl.multiple_of(base + EDGE, EDGE), SPAN)
        for p in range(depth):
            total = product(table, high_ref[p, :, inner_span], low_ref[p, :, inner_span])
            near, far = 0.0, 0.0
            for q in range(depth):
                if abs(q - p) == 1:
                    near = near + mid_ref[q, :, span]
                if abs(q - p) == 2:
                    far = far + mid_ref[q, :, span]
            scale = absorb_ref[pl.ds(p, 1), span] - 90.0 * factor
            out_ref[p, :, span] = (
                total + scale * mid_ref[p, :, span] + factor * (16.0 * near - far)
            )
        for k in range(SPAN // EDGE):
            window = pl.ds(pl.multiple_of(base + k * EDGE, EDGE), SPAN)
            tile = pl.ds(pl.multiple_of(base + k * EDGE, EDGE), EDGE)
            high = jnp.concatenate([high_ref[p, own, window] for p in range(depth)], axis=0)
            low = jnp.concatenate([low_ref[p, own, window] for p in range(depth)], axis=0)
            around = jnp.dot(high, bands_ref[k], preferred_element_type=jnp.float32)
            around = around + jnp.dot(low, bands_ref[k], preferred_element_type=jnp.float32)
            for p in range(depth):
                out_ref[p, :, tile] += factor * around[p * steps : (p + 1) * steps]
        return 0

    lax.fori_loop(0, width // SPAN, one_span, 0)


def local_part(table, bands, field, head, carried, absorption):
    depth, steps, plane = field.shape
    per = TILE // EDGE
    last = plane // EDGE - 1
    cols = table.shape[1]
    wide = (depth, cols, TILE + 2 * EDGE)
    return pl.pallas_call(
        local_kernel,
        out_shape=jax.ShapeDtypeStruct(field.shape, jnp.float32),
        grid=(plane // TILE,),
        in_specs=[
            pl.BlockSpec((steps, cols), lambda i: (0, 0)),
            pl.BlockSpec(bands.shape, lambda i: (0, 0, 0)),
            pl.BlockSpec((depth, steps, EDGE), lambda i: (0, 0, jnp.maximum(i * per - 1, 0))),
            pl.BlockSpec((depth, steps, TILE), lambda i: (0, 0, i)),
            pl.BlockSpec((depth, steps, EDGE), lambda i: (0, 0, jnp.minimum(i * per + per, last))),
            pl.BlockSpec((depth, BAND, TILE), lambda i: (0, 0, i)),
            pl.BlockSpec((depth, cols - steps - BAND, TILE), lambda i: (0, 0, i)),
            pl.BlockSpec((depth, TILE), lambda i: (0, i)),
        ],
        out_specs=pl.BlockSpec((depth, steps, TILE), lambda i: (0, 0, i)),
        scratch_shapes=[pltpu.VMEM(wide, jnp.bfloat16), pltpu.VMEM(wide, jnp.bfloat16)],
        compiler_params=pltpu.CompilerParams(vmem_limit_bytes=44 * MIB),
        cost_estimate=pl.CostEstimate(
            flops=6 * cols * steps * depth * plane,
            bytes_accessed=8 * depth * plane * steps,
            transcendentals=0,
        ),
        name="local_part",
    )(table, bands, field, field, field, head, carried, absorption)


def edge_terms(below, above, depth):
    factor = -DIFFUSION / 12.0
    ends = [None] * depth

    def add(p, value):
        if 0 <= p < depth:
            ends[p] = value if ends[p] is None else ends[p] + value

    add(0, 16.0 * below[1] - below[0])
    add(1, -below[1])
    add(depth - 1, 16.0 * above[0] - above[1])
    add(depth - 2, -above[0])
    return [0.0 if end is None else factor * end for end in ends]


def edge_kernel(image_ref, below_ref, above_ref, out_ref):
    depth = image_ref.shape[0]
    terms = edge_terms((below_ref[0], below_ref[1]), (above_ref[0], above_ref[1]), depth)
    for p in range(depth):
        out_ref[p] = image_ref[p] + terms[p]


def hold_kernel(first, image_ref, out_ref, sem):
    rows = out_ref.shape[1]
    copy = pltpu.make_async_copy(image_ref.at[:, pl.ds(first, rows)], out_ref, sem)
    copy.start()
    copy.wait()


def hold_rows(image, first, rows):
    depth, _, plane = image.shape
    return pl.pallas_call(
        functools.partial(hold_kernel, first),
        out_shape=jax.ShapeDtypeStruct((depth, rows, plane), jnp.float32),
        in_specs=[pl.BlockSpec(memory_space=pl.ANY)],
        out_specs=pl.BlockSpec(memory_space=pltpu.VMEM),
        scratch_shapes=[pltpu.SemaphoreType.DMA(())],
        compiler_params=pltpu.CompilerParams(vmem_limit_bytes=44 * MIB),
        name="hold_rows",
    )(image)


def last_kernel(first, width, image_ref, held_ref, below_ref, above_ref, out_ref, done, sems):
    depth, rows, plane = held_ref.shape
    copies = []
    for j in range(plane // width):
        lanes = pl.ds(j * width, width)
        terms = edge_terms(
            (below_ref[0, :, lanes], below_ref[1, :, lanes]),
            (above_ref[0, :, lanes], above_ref[1, :, lanes]),
            depth,
        )
        for p in range(depth):
            done[p, :, lanes] = held_ref[p, :, lanes] + terms[p]
        copy = pltpu.make_async_copy(
            done.at[:, :, lanes], out_ref.at[:, pl.ds(first, rows), lanes], sems.at[j]
        )
        copy.start()
        copies.append(copy)
    for copy in copies:
        copy.wait()


def add_last(image, held, below, above, first):
    depth, rows, plane = held.shape
    width = TILE
    vmem = pl.BlockSpec(memory_space=pltpu.VMEM)
    return pl.pallas_call(
        functools.partial(last_kernel, first, width),
        out_shape=jax.ShapeDtypeStruct(image.shape, jnp.float32),
        in_specs=[pl.BlockSpec(memory_space=pl.ANY), vmem, vmem, vmem],
        out_specs=pl.BlockSpec(memory_space=pl.ANY),
        scratch_shapes=[
            pltpu.VMEM((depth, rows, plane), jnp.float32),
            pltpu.SemaphoreType.DMA((plane // width,)),
        ],
        input_output_aliases={0: 0},
        compiler_params=pltpu.CompilerParams(vmem_limit_bytes=8 * MIB),
        name="add_last",
    )(image, held, below, above)


def add_edges(image, below, above, first, rows, width):
    depth, _, plane = image.shape
    count = below.shape[1]
    at = first // rows
    return pl.pallas_call(
        edge_kernel,
        out_shape=jax.ShapeDtypeStruct(image.shape, jnp.float32),
        grid=(count // rows, plane // width),
        in_specs=[
            pl.BlockSpec((depth, rows, width), lambda i, j: (0, at + i, j)),
            pl.BlockSpec((2, rows, width), lambda i, j: (0, i, j)),
            pl.BlockSpec((2, rows, width), lambda i, j: (0, i, j)),
        ],
        out_specs=pl.BlockSpec((depth, rows, width), lambda i, j: (0, at + i, j)),
        input_output_aliases={0: 0},
        cost_estimate=pl.CostEstimate(
            flops=8 * depth * count * plane,
            bytes_accessed=4 * count * plane * (2 * depth + 4),
            transcendentals=0,
        ),
        compiler_params=pltpu.CompilerParams(vmem_limit_bytes=16 * MIB),
        name="add_edges",
    )(image, below, above)


def per_device(adjoint_field, absorption, mode_rates, mode_weights):
    steps, depth, plane = adjoint_field.shape
    groups = lax.axis_size("tm")
    slabs = lax.axis_size("space")
    field = jnp.transpose(adjoint_field, (1, 0, 2))

    up = [(i, i + 1) for i in range(slabs - 1)]
    down = [(i + 1, i) for i in range(slabs - 1)]
    below, above, starts = [], [], []
    first = 0
    source = field
    for count in CHUNKS:
        starts.append(first)
        high = source[depth - 2 :, first : first + count]
        low = source[:2, first : first + count]
        below.append(lax.ppermute(high, "space", up))
        above.append(lax.ppermute(low, "space", down))
        source, _, _ = lax.optimization_barrier((source, high, low))
        if len(starts) == 3:
            early = source
        first += count

    scaled = mode_rates / (steps * groups)
    mode_gain = mode_weights * jnp.sqrt(-jnp.expm1(-2.0 * scaled))
    table, projector = history_tables(scaled, mode_gain, steps)

    mine_first = early[:, :BAND]
    head = lax.ppermute(mine_first, "tm", [(g + 1, g) for g in range(groups - 1)])
    sums = block_sums(projector, early)
    decay = jnp.exp(-scaled * steps)[None, :, None]
    swap = [(g, g + 1 - 2 * (g % 2)) for g in range(groups)]
    other = lax.ppermute(sums, "tm", swap)
    core = lax.axis_index("tm") % 2
    half = plane // 2
    mine_half = lax.dynamic_slice_in_dim(sums, core * half, half, axis=2)
    other_half = lax.dynamic_slice_in_dim(other, core * half, half, axis=2)
    pair_half = jnp.where(
        core == 0, mine_half + decay * other_half, other_half + decay * mine_half
    )
    later = None
    for _ in range(groups // 2 - 1):
        sent = pair_half if later is None else pair_half + decay * decay * later
        later = lax.ppermute(sent, "tm", [(g + 2, g) for g in range(groups - 2)])
    later_other = lax.ppermute(later, "tm", swap)
    later_full = jnp.where(
        core == 0,
        jnp.concatenate([later, later_other], axis=2),
        jnp.concatenate([later_other, later], axis=2),
    )
    carried = jnp.where(core == 0, other + decay * later_full, later_full)

    image = local_part(table, stencil_bands(), field, head, carried, absorption)
    held = hold_rows(image, starts[-1], CHUNKS[-1])
    for first, lower, upper in zip(starts[:-1], below, above):
        image = add_edges(image, lower, upper, first, 8, plane)
    image = add_last(image, held, below[-1], above[-1], starts[-1])
    return jnp.transpose(image, (1, 0, 2))


def solution(mesh):
    return jax.shard_map(
        per_device,
        mesh=mesh,
        in_specs=(P("tm", "space", None), P("space", None), P(), P()),
        out_specs=P("tm", "space", None),
        check_vma=False,
    )
```

```python
import functools

import jax
import jax.numpy as jnp
from jax import lax
from jax.experimental import pallas as pl
from jax.experimental.pallas import tpu as pltpu
from jax.sharding import PartitionSpec as P


NY = 96
BAND = 16
DIFFUSION = 0.2
ORDER_EXP = 0.4
EDGE = 256
TILE = 2304
SPAN = 768
MIB = 1024 * 1024
CHUNKS = (8, 24, 64, 24, 8)


def caputo_weights(count):
    steps_idx = jnp.arange(count, dtype=jnp.float32)
    increments = (steps_idx + 1.0) ** ORDER_EXP - steps_idx**ORDER_EXP
    earlier = jnp.concatenate([jnp.zeros((1,), jnp.float32), increments[:-1]])
    return increments - earlier


def history_tables(scaled, mode_gain, steps_dev):
    span_len = steps_dev + BAND
    row_idx = jnp.arange(steps_dev, dtype=jnp.int32)[:, None]
    col_idx = jnp.arange(span_len, dtype=jnp.int32)[None, :]
    lag = col_idx - row_idx
    lag_clip = jnp.clip(lag, 0, span_len).astype(jnp.float32)
    far = jnp.sum(
        mode_gain[:, None, None] * jnp.exp(-scaled[:, None, None] * lag_clip[None]), axis=0
    )
    onehot = (lag[None] == jnp.arange(BAND, dtype=jnp.int32)[:, None, None]).astype(jnp.float32)
    near = jnp.sum(caputo_weights(BAND)[:, None, None] * onehot, axis=0)
    in_band = (lag >= 0) & (lag < BAND)
    own = near + jnp.where(lag >= BAND, far, 0.0)
    ahead = jnp.where(in_band, near - far, 0.0)
    step_pos = jnp.arange(steps_dev, dtype=jnp.float32)
    remote = mode_gain[None, :] * jnp.exp(-scaled[None, :] * (steps_dev - step_pos)[:, None])
    table = jnp.concatenate(
        [jnp.where(col_idx < steps_dev, own, ahead), remote], axis=1
    )
    projector = jnp.exp(-scaled[:, None] * step_pos[None, :])
    return table, projector


def parts(value):
    high = value.astype(jnp.bfloat16)
    return high, (value - high.astype(jnp.float32)).astype(jnp.bfloat16)


def product(weights, high, low):
    rows = weights.shape[0]
    upper, lower = parts(weights)
    both = jnp.dot(
        jnp.concatenate([upper, lower], axis=0), high, preferred_element_type=jnp.float32
    )
    rest = jnp.dot(upper, low, preferred_element_type=jnp.float32)
    return both[:rows] + both[rows:] + rest


def odd_slab():
    return lax.axis_index("space") % 2


def first_cut_kernel(first, field_ref, odd_ref, even_ref, sems):
    depth = field_ref.shape[0]
    rows = pl.ds(first, odd_ref.shape[1])
    up = depth - 2
    parity = odd_slab()
    copies = [
        pltpu.make_async_copy(field_ref.at[pl.ds(parity * up, 2), rows], odd_ref, sems.at[0]),
        pltpu.make_async_copy(field_ref.at[pl.ds((1 - parity) * up, 2), rows], even_ref, sems.at[1]),
    ]
    for copy in copies:
        copy.start()
    for copy in copies:
        copy.wait()


def first_cut(field, first, rows):
    piece = jax.ShapeDtypeStruct((2, rows, field.shape[2]), jnp.float32)
    vmem = pl.BlockSpec(memory_space=pltpu.VMEM)
    return pl.pallas_call(
        functools.partial(first_cut_kernel, first),
        out_shape=(piece, piece),
        in_specs=[pl.BlockSpec(memory_space=pl.ANY)],
        out_specs=(vmem, vmem),
        scratch_shapes=[pltpu.SemaphoreType.DMA((2,))],
        compiler_params=pltpu.CompilerParams(vmem_limit_bytes=46 * MIB),
        name="first_cut",
    )(field)


def cut_kernel(field_ref, odd_ref, even_ref):
    up = field_ref.shape[0] - 2
    parity = odd_slab()
    odd_ref[...] = field_ref[pl.ds(parity * up, 2)]
    even_ref[...] = field_ref[pl.ds((1 - parity) * up, 2)]


def cut(field, first, count):
    depth, _, plane = field.shape
    piece = jax.ShapeDtypeStruct((2, count, plane), jnp.float32)
    block = pl.BlockSpec((2, 8, plane), lambda i: (0, i, 0))
    return pl.pallas_call(
        cut_kernel,
        out_shape=(piece, piece),
        grid=(count // 8,),
        in_specs=[pl.BlockSpec((depth, 8, plane), lambda i: (0, first // 8 + i, 0))],
        out_specs=(block, block),
        compiler_params=pltpu.CompilerParams(vmem_limit_bytes=46 * MIB),
        cost_estimate=pl.CostEstimate(
            flops=0, bytes_accessed=4 * count * plane * (depth + 4), transcendentals=0
        ),
        name="cut",
    )(field)


def project_kernel(projector_ref, field_ref, out_ref):
    high, low = parts(field_ref[0])
    out_ref[0] = product(projector_ref[...], high, low)


def block_sums(projector, field):
    depth, steps, plane = field.shape
    modes = projector.shape[0]
    return pl.pallas_call(
        project_kernel,
        out_shape=jax.ShapeDtypeStruct((depth, modes, plane), jnp.float32),
        grid=(depth, plane // TILE),
        in_specs=[
            pl.BlockSpec((modes, steps), lambda p, i: (0, 0)),
            pl.BlockSpec((1, steps, TILE), lambda p, i: (p, 0, i)),
        ],
        out_specs=pl.BlockSpec((1, modes, TILE), lambda p, i: (p, 0, i)),
        cost_estimate=pl.CostEstimate(
            flops=6 * modes * steps * depth * plane,
            bytes_accessed=4 * depth * plane * (steps + modes),
            transcendentals=0,
        ),
        compiler_params=pltpu.CompilerParams(vmem_limit_bytes=46 * MIB),
        name="block_sums",
    )(projector, field)


def stencil_bands():
    shape = (SPAN // EDGE, SPAN, EDGE)
    lane_out = lax.broadcasted_iota(jnp.int32, shape, 2)
    offset = lax.broadcasted_iota(jnp.int32, shape, 1) - EDGE - lane_out
    column = (lax.broadcasted_iota(jnp.int32, shape, 0) * EDGE + lane_out) % NY
    inside = (column + offset >= 0) & (column + offset < NY)
    size = jnp.abs(offset)
    near = (size == NY) | ((size == 1) & inside)
    far = (size == 2 * NY) | ((size == 2) & inside)
    return jnp.where(near, 16.0, jnp.where(far, -1.0, 0.0)).astype(jnp.bfloat16)


def local_kernel(
    table_ref,
    bands_ref,
    left_ref,
    mid_ref,
    right_ref,
    head_ref,
    carried_ref,
    absorb_ref,
    out_ref,
    high_ref,
    low_ref,
):
    depth, steps, width = mid_ref.shape
    spot, spots = pl.program_id(0), pl.num_programs(0)
    has_left = jnp.where(spot > 0, 1.0, 0.0)
    has_right = jnp.where(spot < spots - 1, 1.0, 0.0)
    factor = -DIFFUSION / 12.0
    table = table_ref[...]

    def put(p, rows, lanes, value):
        high, low = parts(value)
        high_ref[p, rows, lanes] = high
        low_ref[p, rows, lanes] = low

    own, ahead, later = slice(0, steps), slice(steps, steps + BAND), slice(steps + BAND, None)
    inner = slice(EDGE, EDGE + width)
    for p in range(depth):
        put(p, own, slice(0, EDGE), left_ref[p] * has_left)
        put(p, own, inner, mid_ref[p])
        put(p, own, slice(EDGE + width, None), right_ref[p] * has_right)
        put(p, ahead, inner, head_ref[p])
        put(p, later, inner, carried_ref[p])

    def one_span(g, _):
        base = pl.multiple_of(g * SPAN, SPAN)
        span = pl.ds(base, SPAN)
        inner_span = pl.ds(pl.multiple_of(base + EDGE, EDGE), SPAN)
        for p in range(depth):
            total = product(table, high_ref[p, :, inner_span], low_ref[p, :, inner_span])
            near, far = 0.0, 0.0
            for q in range(depth):
                if abs(q - p) == 1:
                    near = near + mid_ref[q, :, span]
                if abs(q - p) == 2:
                    far = far + mid_ref[q, :, span]
            scale = absorb_ref[pl.ds(p, 1), span] - 90.0 * factor
            out_ref[p, :, span] = (
                total + scale * mid_ref[p, :, span] + factor * (16.0 * near - far)
            )
        for k in range(SPAN // EDGE):
            window = pl.ds(pl.multiple_of(base + k * EDGE, EDGE), SPAN)
            tile = pl.ds(pl.multiple_of(base + k * EDGE, EDGE), EDGE)
            high = jnp.concatenate([high_ref[p, own, window] for p in range(depth)], axis=0)
            low = jnp.concatenate([low_ref[p, own, window] for p in range(depth)], axis=0)
            around = jnp.dot(high, bands_ref[k], preferred_element_type=jnp.float32)
            around = around + jnp.dot(low, bands_ref[k], preferred_element_type=jnp.float32)
            for p in range(depth):
                out_ref[p, :, tile] += factor * around[p * steps : (p + 1) * steps]
        return 0

    lax.fori_loop(0, width // SPAN, one_span, 0)


def local_part(table, bands, field, head, carried, absorption):
    depth, steps, plane = field.shape
    per = TILE // EDGE
    last = plane // EDGE - 1
    cols = table.shape[1]
    wide = (depth, cols, TILE + 2 * EDGE)
    return pl.pallas_call(
        local_kernel,
        out_shape=jax.ShapeDtypeStruct(field.shape, jnp.float32),
        grid=(plane // TILE,),
        in_specs=[
            pl.BlockSpec((steps, cols), lambda i: (0, 0)),
            pl.BlockSpec(bands.shape, lambda i: (0, 0, 0)),
            pl.BlockSpec((depth, steps, EDGE), lambda i: (0, 0, jnp.maximum(i * per - 1, 0))),
            pl.BlockSpec((depth, steps, TILE), lambda i: (0, 0, i)),
            pl.BlockSpec((depth, steps, EDGE), lambda i: (0, 0, jnp.minimum(i * per + per, last))),
            pl.BlockSpec((depth, BAND, TILE), lambda i: (0, 0, i)),
            pl.BlockSpec((depth, cols - steps - BAND, TILE), lambda i: (0, 0, i)),
            pl.BlockSpec((depth, TILE), lambda i: (0, i)),
        ],
        out_specs=pl.BlockSpec((depth, steps, TILE), lambda i: (0, 0, i)),
        scratch_shapes=[pltpu.VMEM(wide, jnp.bfloat16), pltpu.VMEM(wide, jnp.bfloat16)],
        compiler_params=pltpu.CompilerParams(vmem_limit_bytes=44 * MIB),
        cost_estimate=pl.CostEstimate(
            flops=6 * cols * steps * depth * plane,
            bytes_accessed=8 * depth * plane * steps,
            transcendentals=0,
        ),
        name="local_part",
    )(table, bands, field, field, field, head, carried, absorption)


def edge_terms(below, above, depth):
    factor = -DIFFUSION / 12.0
    ends = [None] * depth

    def add(p, value):
        if 0 <= p < depth:
            ends[p] = value if ends[p] is None else ends[p] + value

    add(0, 16.0 * below[1] - below[0])
    add(1, -below[1])
    add(depth - 1, 16.0 * above[0] - above[1])
    add(depth - 2, -above[0])
    return [0.0 if end is None else factor * end for end in ends]


def by_side(odd, even):
    lower = odd_slab() == 0
    below = [jnp.where(lower, odd[k], even[k]) for k in range(2)]
    above = [jnp.where(lower, even[k], odd[k]) for k in range(2)]
    return below, above


def edge_kernel(image_ref, odd_ref, even_ref, out_ref):
    depth = image_ref.shape[0]
    below, above = by_side(odd_ref, even_ref)
    terms = edge_terms(below, above, depth)
    for p in range(depth):
        out_ref[p] = image_ref[p] + terms[p]


def hold_kernel(first, image_ref, out_ref, sem):
    rows = out_ref.shape[1]
    copy = pltpu.make_async_copy(image_ref.at[:, pl.ds(first, rows)], out_ref, sem)
    copy.start()
    copy.wait()


def hold_rows(image, first, rows):
    depth, _, plane = image.shape
    return pl.pallas_call(
        functools.partial(hold_kernel, first),
        out_shape=jax.ShapeDtypeStruct((depth, rows, plane), jnp.float32),
        in_specs=[pl.BlockSpec(memory_space=pl.ANY)],
        out_specs=pl.BlockSpec(memory_space=pltpu.VMEM),
        scratch_shapes=[pltpu.SemaphoreType.DMA(())],
        compiler_params=pltpu.CompilerParams(vmem_limit_bytes=44 * MIB),
        name="hold_rows",
    )(image)


def last_kernel(first, width, image_ref, held_ref, odd_ref, even_ref, out_ref, done, sems):
    depth, rows, plane = held_ref.shape
    stores = []
    for j in range(plane // width):
        lanes = pl.ds(j * width, width)
        below, above = by_side(odd_ref[:, :, lanes], even_ref[:, :, lanes])
        terms = edge_terms(below, above, depth)
        for p in range(depth):
            done[p, :, lanes] = held_ref[p, :, lanes] + terms[p]
        store = pltpu.make_async_copy(
            done.at[:, :, lanes], out_ref.at[:, pl.ds(first, rows), lanes], sems.at[j]
        )
        store.start()
        stores.append(store)
    for store in stores:
        store.wait()


def add_last(image, held, odd, even, first):
    depth, rows, plane = held.shape
    width = TILE
    anywhere = pl.BlockSpec(memory_space=pl.ANY)
    vmem = pl.BlockSpec(memory_space=pltpu.VMEM)
    return pl.pallas_call(
        functools.partial(last_kernel, first, width),
        out_shape=jax.ShapeDtypeStruct(image.shape, jnp.float32),
        in_specs=[anywhere, vmem, vmem, vmem],
        out_specs=anywhere,
        scratch_shapes=[
            pltpu.VMEM((depth, rows, plane), jnp.float32),
            pltpu.SemaphoreType.DMA((plane // width,)),
        ],
        input_output_aliases={0: 0},
        compiler_params=pltpu.CompilerParams(vmem_limit_bytes=8 * MIB),
        name="add_last",
    )(image, held, odd, even)


def add_edges(image, odd, even, first, rows, width):
    depth, _, plane = image.shape
    count = odd.shape[1]
    at = first // rows
    return pl.pallas_call(
        edge_kernel,
        out_shape=jax.ShapeDtypeStruct(image.shape, jnp.float32),
        grid=(count // rows, plane // width),
        in_specs=[
            pl.BlockSpec((depth, rows, width), lambda i, j: (0, at + i, j)),
            pl.BlockSpec((2, rows, width), lambda i, j: (0, i, j)),
            pl.BlockSpec((2, rows, width), lambda i, j: (0, i, j)),
        ],
        out_specs=pl.BlockSpec((depth, rows, width), lambda i, j: (0, at + i, j)),
        input_output_aliases={0: 0},
        cost_estimate=pl.CostEstimate(
            flops=8 * depth * count * plane,
            bytes_accessed=4 * count * plane * (2 * depth + 4),
            transcendentals=0,
        ),
        compiler_params=pltpu.CompilerParams(vmem_limit_bytes=16 * MIB),
        name="add_edges",
    )(image, odd, even)


def per_device(adjoint_field, absorption, mode_rates, mode_weights):
    steps, _, plane = adjoint_field.shape
    groups = lax.axis_size("tm")
    slabs = lax.axis_size("space")
    field = jnp.transpose(adjoint_field, (1, 0, 2))

    def both_ways(lowest):
        pairs = [(i, i + 1) for i in range(lowest, slabs - 1, 2)]
        return pairs + [(j, i) for i, j in pairs]

    odds, evens, starts = [], [], []
    first = 0
    source = field
    for k, count in enumerate(CHUNKS):
        starts.append(first)
        over_odd, over_even = (first_cut if k == 0 else cut)(source, first, count)
        odds.append(lax.ppermute(over_odd, "space", both_ways(1)))
        evens.append(lax.ppermute(over_even, "space", both_ways(0)))
        source, _, _ = lax.optimization_barrier((source, over_odd, over_even))
        if len(starts) == 3:
            early, odds[0], evens[0] = lax.optimization_barrier((source, odds[0], evens[0]))
        first += count

    scaled = mode_rates / (steps * groups)
    mode_gain = mode_weights * jnp.sqrt(-jnp.expm1(-2.0 * scaled))
    table, projector = history_tables(scaled, mode_gain, steps)

    mine_first = early[:, :BAND]
    head = lax.ppermute(mine_first, "tm", [(g + 1, g) for g in range(groups - 1)])
    sums = block_sums(projector, early)
    decay = jnp.exp(-scaled * steps)[None, :, None]
    swap = [(g, g + 1 - 2 * (g % 2)) for g in range(groups)]
    other = lax.ppermute(sums, "tm", swap)
    core = lax.axis_index("tm") % 2
    half = plane // 2
    mine_half = lax.dynamic_slice_in_dim(sums, core * half, half, axis=2)
    other_half = lax.dynamic_slice_in_dim(other, core * half, half, axis=2)
    pair_half = jnp.where(
        core == 0, mine_half + decay * other_half, other_half + decay * mine_half
    )
    later = None
    for _ in range(groups // 2 - 1):
        sent = pair_half if later is None else pair_half + decay * decay * later
        later = lax.ppermute(sent, "tm", [(g + 2, g) for g in range(groups - 2)])
    later_other = lax.ppermute(later, "tm", swap)
    later_full = jnp.where(
        core == 0,
        jnp.concatenate([later, later_other], axis=2),
        jnp.concatenate([later_other, later], axis=2),
    )
    carried = jnp.where(core == 0, other + decay * later_full, later_full)

    image = local_part(table, stencil_bands(), field, head, carried, absorption)
    held = hold_rows(image, starts[-1], CHUNKS[-1])
    for first, lower, upper in zip(starts[:-1], odds, evens):
        image = add_edges(image, lower, upper, first, 8, plane)
    image = add_last(image, held, odds[-1], evens[-1], starts[-1])
    return jnp.transpose(image, (1, 0, 2))


def solution(mesh):
    return jax.shard_map(
        per_device,
        mesh=mesh,
        in_specs=(P("tm", "space", None), P("space", None), P(), P()),
        out_specs=P("tm", "space", None),
        check_vma=False,
    )
```

```python
import functools

import jax
import jax.numpy as jnp
from jax import lax
from jax.experimental import pallas as pl
from jax.experimental.pallas import tpu as pltpu
from jax.sharding import PartitionSpec as P


NY = 96
BAND = 16
DIFFUSION = 0.2
ORDER_EXP = 0.4
EDGE = 256
TILE = 2304
SPAN = 768
MIB = 1024 * 1024
PIECES = 4
CHUNKS = (16, 24, 56, 24, 8)


def caputo_weights(count):
    steps_idx = jnp.arange(count, dtype=jnp.float32)
    increments = (steps_idx + 1.0) ** ORDER_EXP - steps_idx**ORDER_EXP
    earlier = jnp.concatenate([jnp.zeros((1,), jnp.float32), increments[:-1]])
    return increments - earlier


def history_tables(scaled, mode_gain, steps_dev):
    span_len = steps_dev + BAND
    row_idx = jnp.arange(steps_dev, dtype=jnp.int32)[:, None]
    col_idx = jnp.arange(span_len, dtype=jnp.int32)[None, :]
    lag = col_idx - row_idx
    lag_clip = jnp.clip(lag, 0, span_len).astype(jnp.float32)
    far = jnp.sum(
        mode_gain[:, None, None] * jnp.exp(-scaled[:, None, None] * lag_clip[None]), axis=0
    )
    onehot = (lag[None] == jnp.arange(BAND, dtype=jnp.int32)[:, None, None]).astype(jnp.float32)
    near = jnp.sum(caputo_weights(BAND)[:, None, None] * onehot, axis=0)
    in_band = (lag >= 0) & (lag < BAND)
    own = near + jnp.where(lag >= BAND, far, 0.0)
    ahead = jnp.where(in_band, near - far, 0.0)
    step_pos = jnp.arange(steps_dev, dtype=jnp.float32)
    remote = mode_gain[None, :] * jnp.exp(-scaled[None, :] * (steps_dev - step_pos)[:, None])
    table = jnp.concatenate(
        [jnp.where(col_idx < steps_dev, own, ahead), remote], axis=1
    )
    projector = jnp.exp(-scaled[:, None] * step_pos[None, :])
    return table, projector


def parts(value):
    high = value.astype(jnp.bfloat16)
    return high, (value - high.astype(jnp.float32)).astype(jnp.bfloat16)


def product(weights, high, low):
    rows = weights.shape[0]
    upper, lower = parts(weights)
    both = jnp.dot(
        jnp.concatenate([upper, lower], axis=0), high, preferred_element_type=jnp.float32
    )
    rest = jnp.dot(upper, low, preferred_element_type=jnp.float32)
    return both[:rows] + both[rows:] + rest


def odd_slab():
    return lax.axis_index("space") % 2


def lead_kernel(
    first,
    slabs,
    field_ref,
    below_ref,
    above_ref,
    odd_ref,
    even_ref,
    zero,
    planes,
    send_sems,
    recv_sems,
    local_sems,
    turn,
):
    depth = field_ref.shape[0]
    rows, plane = below_ref.shape[1:]
    width = plane // PIECES
    slab, group = lax.axis_index("space"), lax.axis_index("tm")
    core = group % 2
    partner = group + 1 - 2 * core
    has_up, has_down = slab < slabs - 1, slab > 0
    mesh_id = pl.DeviceIdType.MESH

    barrier = pltpu.get_barrier_semaphore()
    pl.semaphore_signal(barrier, inc=1, device_id={"tm": partner}, device_id_type=mesh_id)

    @pl.when(has_up)
    def _():
        pl.semaphore_signal(barrier, inc=1, device_id={"space": slab + 1}, device_id_type=mesh_id)

    @pl.when(has_down)
    def _():
        pl.semaphore_signal(barrier, inc=1, device_id={"space": slab - 1}, device_id_type=mesh_id)

    pl.semaphore_wait(barrier, 1 + has_up.astype(jnp.int32) + has_down.astype(jnp.int32))

    def piece(way, j):
        lanes = pl.ds(j * width, width)
        start, target, step = ((depth - 2, below_ref, 1), (0, above_ref, -1))[way]
        return pltpu.make_async_remote_copy(
            src_ref=field_ref.at[pl.ds(start, 2), pl.ds(0, rows), lanes],
            dst_ref=target.at[:, :, lanes],
            send_sem=send_sems.at[way, j],
            recv_sem=recv_sems.at[way, j],
            device_id={"space": slab + step},
            device_id_type=mesh_id,
        )

    def on_both(act, pieces):
        for way, has in ((0, has_up), (1, has_down)):

            @pl.when(has)
            def _(way=way):
                for j in pieces:
                    act(piece(way, j))

    @pl.when(core == 0)
    def _():
        on_both(lambda copy: copy.start(), range(PIECES))

    count = odd_ref.shape[1]
    load = pltpu.make_async_copy(field_ref.at[:, pl.ds(first, count)], planes, local_sems.at[0])
    load.start()
    zero[...] = jnp.zeros_like(zero)
    load.wait()
    parity = odd_slab()
    up = depth - 2
    stores = [
        pltpu.make_async_copy(planes.at[pl.ds(parity * up, 2)], odd_ref, local_sems.at[1]),
        pltpu.make_async_copy(planes.at[pl.ds((1 - parity) * up, 2)], even_ref, local_sems.at[2]),
    ]
    for store in stores:
        store.start()
    for store in stores:
        store.wait()

    @pl.when(core == 0)
    def _():
        on_both(lambda copy: copy.wait_send(), range(PIECES - 1))
        pl.semaphore_signal(turn, inc=1, device_id={"tm": partner}, device_id_type=mesh_id)
        on_both(lambda copy: copy.wait_send(), range(PIECES - 1, PIECES))

    @pl.when(core == 1)
    def _():
        pl.semaphore_wait(turn, 1)
        on_both(lambda copy: copy.start(), range(PIECES))
        on_both(lambda copy: copy.wait_send(), range(PIECES))

    for has, way, target in ((has_down, 0, below_ref), (has_up, 1, above_ref)):

        @pl.when(has)
        def _(way=way):
            for j in range(PIECES):
                piece(way, j).wait_recv()

        @pl.when(jnp.logical_not(has))
        def _(target=target):
            fill = pltpu.make_async_copy(zero, target, local_sems.at[0])
            fill.start()
            fill.wait()


def lead(field, rows, first, count, slabs):
    depth, _, plane = field.shape
    arrived = jax.ShapeDtypeStruct((2, rows, plane), jnp.float32)
    piece = jax.ShapeDtypeStruct((2, count, plane), jnp.float32)
    anywhere = pl.BlockSpec(memory_space=pl.ANY)
    return pl.pallas_call(
        functools.partial(lead_kernel, first, slabs),
        out_shape=(arrived, arrived, piece, piece),
        in_specs=[anywhere],
        out_specs=(anywhere,) * 4,
        scratch_shapes=[
            pltpu.VMEM((2, rows, plane), jnp.float32),
            pltpu.VMEM((depth, count, plane), jnp.float32),
            pltpu.SemaphoreType.DMA((2, PIECES)),
            pltpu.SemaphoreType.DMA((2, PIECES)),
            pltpu.SemaphoreType.DMA((3,)),
            pltpu.SemaphoreType.REGULAR,
        ],
        compiler_params=pltpu.CompilerParams(
            collective_id=0, has_side_effects=True, vmem_limit_bytes=50 * MIB
        ),
        name="lead",
    )(field)


def cut_kernel(field_ref, odd_ref, even_ref):
    up = field_ref.shape[0] - 2
    parity = odd_slab()
    odd_ref[...] = field_ref[pl.ds(parity * up, 2)]
    even_ref[...] = field_ref[pl.ds((1 - parity) * up, 2)]


def cut(field, first, count):
    depth, _, plane = field.shape
    piece = jax.ShapeDtypeStruct((2, count, plane), jnp.float32)
    block = pl.BlockSpec((2, 8, plane), lambda i: (0, i, 0))
    return pl.pallas_call(
        cut_kernel,
        out_shape=(piece, piece),
        grid=(count // 8,),
        in_specs=[pl.BlockSpec((depth, 8, plane), lambda i: (0, first // 8 + i, 0))],
        out_specs=(block, block),
        compiler_params=pltpu.CompilerParams(vmem_limit_bytes=46 * MIB),
        cost_estimate=pl.CostEstimate(
            flops=0, bytes_accessed=4 * count * plane * (depth + 4), transcendentals=0
        ),
        name="cut",
    )(field)


def project_kernel(projector_ref, field_ref, out_ref):
    high, low = parts(field_ref[0])
    out_ref[0] = product(projector_ref[...], high, low)


def block_sums(projector, field):
    depth, steps, plane = field.shape
    modes = projector.shape[0]
    return pl.pallas_call(
        project_kernel,
        out_shape=jax.ShapeDtypeStruct((depth, modes, plane), jnp.float32),
        grid=(depth, plane // TILE),
        in_specs=[
            pl.BlockSpec((modes, steps), lambda p, i: (0, 0)),
            pl.BlockSpec((1, steps, TILE), lambda p, i: (p, 0, i)),
        ],
        out_specs=pl.BlockSpec((1, modes, TILE), lambda p, i: (p, 0, i)),
        cost_estimate=pl.CostEstimate(
            flops=6 * modes * steps * depth * plane,
            bytes_accessed=4 * depth * plane * (steps + modes),
            transcendentals=0,
        ),
        compiler_params=pltpu.CompilerParams(vmem_limit_bytes=46 * MIB),
        name="block_sums",
    )(projector, field)


def stencil_bands():
    shape = (SPAN // EDGE, SPAN, EDGE)
    lane_out = lax.broadcasted_iota(jnp.int32, shape, 2)
    offset = lax.broadcasted_iota(jnp.int32, shape, 1) - EDGE - lane_out
    column = (lax.broadcasted_iota(jnp.int32, shape, 0) * EDGE + lane_out) % NY
    inside = (column + offset >= 0) & (column + offset < NY)
    size = jnp.abs(offset)
    near = (size == NY) | ((size == 1) & inside)
    far = (size == 2 * NY) | ((size == 2) & inside)
    return jnp.where(near, 16.0, jnp.where(far, -1.0, 0.0)).astype(jnp.bfloat16)


def local_kernel(
    table_ref,
    bands_ref,
    left_ref,
    mid_ref,
    right_ref,
    head_ref,
    carried_ref,
    absorb_ref,
    out_ref,
    high_ref,
    low_ref,
):
    depth, steps, width = mid_ref.shape
    spot, spots = pl.program_id(0), pl.num_programs(0)
    has_left = jnp.where(spot > 0, 1.0, 0.0)
    has_right = jnp.where(spot < spots - 1, 1.0, 0.0)
    factor = -DIFFUSION / 12.0
    table = table_ref[...]

    def put(p, rows, lanes, value):
        high, low = parts(value)
        high_ref[p, rows, lanes] = high
        low_ref[p, rows, lanes] = low

    own, ahead, later = slice(0, steps), slice(steps, steps + BAND), slice(steps + BAND, None)
    inner = slice(EDGE, EDGE + width)
    for p in range(depth):
        put(p, own, slice(0, EDGE), left_ref[p] * has_left)
        put(p, own, inner, mid_ref[p])
        put(p, own, slice(EDGE + width, None), right_ref[p] * has_right)
        put(p, ahead, inner, head_ref[p])
        put(p, later, inner, carried_ref[p])

    def one_span(g, _):
        base = pl.multiple_of(g * SPAN, SPAN)
        span = pl.ds(base, SPAN)
        inner_span = pl.ds(pl.multiple_of(base + EDGE, EDGE), SPAN)
        for p in range(depth):
            total = product(table, high_ref[p, :, inner_span], low_ref[p, :, inner_span])
            near, far = 0.0, 0.0
            for q in range(depth):
                if abs(q - p) == 1:
                    near = near + mid_ref[q, :, span]
                if abs(q - p) == 2:
                    far = far + mid_ref[q, :, span]
            scale = absorb_ref[pl.ds(p, 1), span] - 90.0 * factor
            out_ref[p, :, span] = (
                total + scale * mid_ref[p, :, span] + factor * (16.0 * near - far)
            )
        for k in range(SPAN // EDGE):
            window = pl.ds(pl.multiple_of(base + k * EDGE, EDGE), SPAN)
            tile = pl.ds(pl.multiple_of(base + k * EDGE, EDGE), EDGE)
            high = jnp.concatenate([high_ref[p, own, window] for p in range(depth)], axis=0)
            low = jnp.concatenate([low_ref[p, own, window] for p in range(depth)], axis=0)
            around = jnp.dot(high, bands_ref[k], preferred_element_type=jnp.float32)
            around = around + jnp.dot(low, bands_ref[k], preferred_element_type=jnp.float32)
            for p in range(depth):
                out_ref[p, :, tile] += factor * around[p * steps : (p + 1) * steps]
        return 0

    lax.fori_loop(0, width // SPAN, one_span, 0)


def local_part(table, bands, field, head, carried, absorption):
    depth, steps, plane = field.shape
    per = TILE // EDGE
    last = plane // EDGE - 1
    cols = table.shape[1]
    wide = (depth, cols, TILE + 2 * EDGE)
    return pl.pallas_call(
        local_kernel,
        out_shape=jax.ShapeDtypeStruct(field.shape, jnp.float32),
        grid=(plane // TILE,),
        in_specs=[
            pl.BlockSpec((steps, cols), lambda i: (0, 0)),
            pl.BlockSpec(bands.shape, lambda i: (0, 0, 0)),
            pl.BlockSpec((depth, steps, EDGE), lambda i: (0, 0, jnp.maximum(i * per - 1, 0))),
            pl.BlockSpec((depth, steps, TILE), lambda i: (0, 0, i)),
            pl.BlockSpec((depth, steps, EDGE), lambda i: (0, 0, jnp.minimum(i * per + per, last))),
            pl.BlockSpec((depth, BAND, TILE), lambda i: (0, 0, i)),
            pl.BlockSpec((depth, cols - steps - BAND, TILE), lambda i: (0, 0, i)),
            pl.BlockSpec((depth, TILE), lambda i: (0, i)),
        ],
        out_specs=pl.BlockSpec((depth, steps, TILE), lambda i: (0, 0, i)),
        scratch_shapes=[pltpu.VMEM(wide, jnp.bfloat16), pltpu.VMEM(wide, jnp.bfloat16)],
        compiler_params=pltpu.CompilerParams(vmem_limit_bytes=44 * MIB),
        cost_estimate=pl.CostEstimate(
            flops=6 * cols * steps * depth * plane,
            bytes_accessed=8 * depth * plane * steps,
            transcendentals=0,
        ),
        name="local_part",
    )(table, bands, field, field, field, head, carried, absorption)


def edge_terms(below, above, depth):
    factor = -DIFFUSION / 12.0
    ends = [None] * depth

    def add(p, value):
        if 0 <= p < depth:
            ends[p] = value if ends[p] is None else ends[p] + value

    add(0, 16.0 * below[1] - below[0])
    add(1, -below[1])
    add(depth - 1, 16.0 * above[0] - above[1])
    add(depth - 2, -above[0])
    return [0.0 if end is None else factor * end for end in ends]


def by_side(odd, even):
    lower = odd_slab() == 0
    below = [jnp.where(lower, odd[k], even[k]) for k in range(2)]
    above = [jnp.where(lower, even[k], odd[k]) for k in range(2)]
    return below, above


def edge_kernel(sided, image_ref, one_ref, other_ref, out_ref):
    depth = image_ref.shape[0]
    below, above = (one_ref, other_ref) if sided else by_side(one_ref, other_ref)
    terms = edge_terms(below, above, depth)
    for p in range(depth):
        out_ref[p] = image_ref[p] + terms[p]


def hold_kernel(first, image_ref, out_ref, sem):
    rows = out_ref.shape[1]
    copy = pltpu.make_async_copy(image_ref.at[:, pl.ds(first, rows)], out_ref, sem)
    copy.start()
    copy.wait()


def hold_rows(image, first, rows):
    depth, _, plane = image.shape
    return pl.pallas_call(
        functools.partial(hold_kernel, first),
        out_shape=jax.ShapeDtypeStruct((depth, rows, plane), jnp.float32),
        in_specs=[pl.BlockSpec(memory_space=pl.ANY)],
        out_specs=pl.BlockSpec(memory_space=pltpu.VMEM),
        scratch_shapes=[pltpu.SemaphoreType.DMA(())],
        compiler_params=pltpu.CompilerParams(vmem_limit_bytes=44 * MIB),
        name="hold_rows",
    )(image)


def last_kernel(first, width, image_ref, held_ref, odd_ref, even_ref, out_ref, done, sems):
    depth, rows, plane = held_ref.shape
    stores = []
    for j in range(plane // width):
        lanes = pl.ds(j * width, width)
        below, above = by_side(odd_ref[:, :, lanes], even_ref[:, :, lanes])
        terms = edge_terms(below, above, depth)
        for p in range(depth):
            done[p, :, lanes] = held_ref[p, :, lanes] + terms[p]
        store = pltpu.make_async_copy(
            done.at[:, :, lanes], out_ref.at[:, pl.ds(first, rows), lanes], sems.at[j]
        )
        store.start()
        stores.append(store)
    for store in stores:
        store.wait()


def add_last(image, held, odd, even, first):
    depth, rows, plane = held.shape
    width = TILE
    anywhere = pl.BlockSpec(memory_space=pl.ANY)
    vmem = pl.BlockSpec(memory_space=pltpu.VMEM)
    return pl.pallas_call(
        functools.partial(last_kernel, first, width),
        out_shape=jax.ShapeDtypeStruct(image.shape, jnp.float32),
        in_specs=[anywhere, vmem, vmem, vmem],
        out_specs=anywhere,
        scratch_shapes=[
            pltpu.VMEM((depth, rows, plane), jnp.float32),
            pltpu.SemaphoreType.DMA((plane // width,)),
        ],
        input_output_aliases={0: 0},
        compiler_params=pltpu.CompilerParams(vmem_limit_bytes=8 * MIB),
        name="add_last",
    )(image, held, odd, even)


def add_edges(image, one, other, first, rows, width, sided=False):
    depth, _, plane = image.shape
    count = one.shape[1]
    at = first // rows
    return pl.pallas_call(
        functools.partial(edge_kernel, sided),
        out_shape=jax.ShapeDtypeStruct(image.shape, jnp.float32),
        grid=(count // rows, plane // width),
        in_specs=[
            pl.BlockSpec((depth, rows, width), lambda i, j: (0, at + i, j)),
            pl.BlockSpec((2, rows, width), lambda i, j: (0, i, j)),
            pl.BlockSpec((2, rows, width), lambda i, j: (0, i, j)),
        ],
        out_specs=pl.BlockSpec((depth, rows, width), lambda i, j: (0, at + i, j)),
        input_output_aliases={0: 0},
        cost_estimate=pl.CostEstimate(
            flops=8 * depth * count * plane,
            bytes_accessed=4 * count * plane * (2 * depth + 4),
            transcendentals=0,
        ),
        compiler_params=pltpu.CompilerParams(vmem_limit_bytes=16 * MIB),
        name="add_edges",
    )(image, one, other)


def per_device(adjoint_field, absorption, mode_rates, mode_weights):
    steps, _, plane = adjoint_field.shape
    groups = lax.axis_size("tm")
    slabs = lax.axis_size("space")
    field = jnp.transpose(adjoint_field, (1, 0, 2))

    def both_ways(lowest):
        pairs = [(i, i + 1) for i in range(lowest, slabs - 1, 2)]
        return pairs + [(j, i) for i, j in pairs]

    starts = [sum(CHUNKS[:k]) for k in range(len(CHUNKS))]
    below, above, over_odd, over_even = lead(field, CHUNKS[0], CHUNKS[0], CHUNKS[1], slabs)
    odds, evens = [], []
    source = field
    for k, count in enumerate(CHUNKS[1:], 1):
        if k > 1:
            over_odd, over_even = cut(source, starts[k], count)
        odds.append(lax.ppermute(over_odd, "space", both_ways(1)))
        evens.append(lax.ppermute(over_even, "space", both_ways(0)))
        source, _, _ = lax.optimization_barrier((source, over_odd, over_even))
        if k == 2:
            early = source

    scaled = mode_rates / (steps * groups)
    mode_gain = mode_weights * jnp.sqrt(-jnp.expm1(-2.0 * scaled))
    table, projector = history_tables(scaled, mode_gain, steps)

    mine_first = early[:, :BAND]
    head = lax.ppermute(mine_first, "tm", [(g + 1, g) for g in range(groups - 1)])
    sums = block_sums(projector, early)
    decay = jnp.exp(-scaled * steps)[None, :, None]
    swap = [(g, g + 1 - 2 * (g % 2)) for g in range(groups)]
    other = lax.ppermute(sums, "tm", swap)
    core = lax.axis_index("tm") % 2
    half = plane // 2
    mine_half = lax.dynamic_slice_in_dim(sums, core * half, half, axis=2)
    other_half = lax.dynamic_slice_in_dim(other, core * half, half, axis=2)
    pair_half = jnp.where(
        core == 0, mine_half + decay * other_half, other_half + decay * mine_half
    )
    later = None
    for _ in range(groups // 2 - 1):
        sent = pair_half if later is None else pair_half + decay * decay * later
        later = lax.ppermute(sent, "tm", [(g + 2, g) for g in range(groups - 2)])
    later_other = lax.ppermute(later, "tm", swap)
    later_full = jnp.where(
        core == 0,
        jnp.concatenate([later, later_other], axis=2),
        jnp.concatenate([later_other, later], axis=2),
    )
    carried = jnp.where(core == 0, other + decay * later_full, later_full)

    image = local_part(table, stencil_bands(), field, head, carried, absorption)
    held = hold_rows(image, starts[-1], CHUNKS[-1])
    image = add_edges(image, below, above, 0, 8, plane, sided=True)
    for k in range(1, len(CHUNKS) - 1):
        image = add_edges(image, odds[k - 1], evens[k - 1], starts[k], 8, plane)
    image = add_last(image, held, odds[-1], evens[-1], starts[-1])
    return jnp.transpose(image, (1, 0, 2))


def solution(mesh):
    return jax.shard_map(
        per_device,
        mesh=mesh,
        in_specs=(P("tm", "space", None), P("space", None), P(), P()),
        out_specs=P("tm", "space", None),
        check_vma=False,
    )
```

```python
import functools

import jax
import jax.numpy as jnp
from jax import lax
from jax.experimental import pallas as pl
from jax.experimental.pallas import tpu as pltpu
from jax.sharding import PartitionSpec as P


NY = 96
BAND = 16
DIFFUSION = 0.2
ORDER_EXP = 0.4
EDGE = 256
TILE = 2304
SPAN = 768
MIB = 1024 * 1024
PIECES = 4
CHUNKS = (16, 32, 48, 24, 8)


def caputo_weights(count):
    steps_idx = jnp.arange(count, dtype=jnp.float32)
    increments = (steps_idx + 1.0) ** ORDER_EXP - steps_idx**ORDER_EXP
    earlier = jnp.concatenate([jnp.zeros((1,), jnp.float32), increments[:-1]])
    return increments - earlier


def history_tables(scaled, mode_gain, steps_dev):
    span_len = steps_dev + BAND
    row_idx = jnp.arange(steps_dev, dtype=jnp.int32)[:, None]
    col_idx = jnp.arange(span_len, dtype=jnp.int32)[None, :]
    lag = col_idx - row_idx
    lag_clip = jnp.clip(lag, 0, span_len).astype(jnp.float32)
    far = jnp.sum(
        mode_gain[:, None, None] * jnp.exp(-scaled[:, None, None] * lag_clip[None]), axis=0
    )
    onehot = (lag[None] == jnp.arange(BAND, dtype=jnp.int32)[:, None, None]).astype(jnp.float32)
    near = jnp.sum(caputo_weights(BAND)[:, None, None] * onehot, axis=0)
    in_band = (lag >= 0) & (lag < BAND)
    own = near + jnp.where(lag >= BAND, far, 0.0)
    ahead = jnp.where(in_band, near - far, 0.0)
    step_pos = jnp.arange(steps_dev, dtype=jnp.float32)
    remote = mode_gain[None, :] * jnp.exp(-scaled[None, :] * (steps_dev - step_pos)[:, None])
    table = jnp.concatenate(
        [jnp.where(col_idx < steps_dev, own, ahead), remote], axis=1
    )
    projector = jnp.exp(-scaled[:, None] * step_pos[None, :])
    return table, projector


def parts(value):
    high = value.astype(jnp.bfloat16)
    return high, (value - high.astype(jnp.float32)).astype(jnp.bfloat16)


def product(weights, high, low):
    rows = weights.shape[0]
    upper, lower = parts(weights)
    both = jnp.dot(
        jnp.concatenate([upper, lower], axis=0), high, preferred_element_type=jnp.float32
    )
    rest = jnp.dot(upper, low, preferred_element_type=jnp.float32)
    return both[:rows] + both[rows:] + rest


def odd_slab():
    return lax.axis_index("space") % 2


def lead_kernel(
    first,
    slabs,
    field_ref,
    below_ref,
    above_ref,
    odd_ref,
    even_ref,
    zero,
    planes,
    send_sems,
    recv_sems,
    local_sems,
    turn,
):
    depth = field_ref.shape[0]
    rows, plane = below_ref.shape[1:]
    width = plane // PIECES
    slab, group = lax.axis_index("space"), lax.axis_index("tm")
    core = group % 2
    partner = group + 1 - 2 * core
    has_up, has_down = slab < slabs - 1, slab > 0
    mesh_id = pl.DeviceIdType.MESH

    barrier = pltpu.get_barrier_semaphore()
    pl.semaphore_signal(barrier, inc=1, device_id={"tm": partner}, device_id_type=mesh_id)

    @pl.when(has_up)
    def _():
        pl.semaphore_signal(barrier, inc=1, device_id={"space": slab + 1}, device_id_type=mesh_id)

    @pl.when(has_down)
    def _():
        pl.semaphore_signal(barrier, inc=1, device_id={"space": slab - 1}, device_id_type=mesh_id)

    pl.semaphore_wait(barrier, 1 + has_up.astype(jnp.int32) + has_down.astype(jnp.int32))

    def piece(way, j):
        lanes = pl.ds(j * width, width)
        start, target, step = ((depth - 2, below_ref, 1), (0, above_ref, -1))[way]
        return pltpu.make_async_remote_copy(
            src_ref=field_ref.at[pl.ds(start, 2), pl.ds(0, rows), lanes],
            dst_ref=target.at[:, :, lanes],
            send_sem=send_sems.at[way, j],
            recv_sem=recv_sems.at[way, j],
            device_id={"space": slab + step},
            device_id_type=mesh_id,
        )

    def on_both(act, pieces):
        for way, has in ((0, has_up), (1, has_down)):

            @pl.when(has)
            def _(way=way):
                for j in pieces:
                    act(piece(way, j))

    @pl.when(core == 0)
    def _():
        on_both(lambda copy: copy.start(), range(PIECES))

    count = odd_ref.shape[1]
    load = pltpu.make_async_copy(field_ref.at[:, pl.ds(first, count)], planes, local_sems.at[0])
    load.start()
    zero[...] = jnp.zeros_like(zero)
    load.wait()
    parity = odd_slab()
    up = depth - 2
    stores = [
        pltpu.make_async_copy(planes.at[pl.ds(parity * up, 2)], odd_ref, local_sems.at[1]),
        pltpu.make_async_copy(planes.at[pl.ds((1 - parity) * up, 2)], even_ref, local_sems.at[2]),
    ]
    for store in stores:
        store.start()
    for store in stores:
        store.wait()

    @pl.when(core == 0)
    def _():
        on_both(lambda copy: copy.wait_send(), range(PIECES - 1))
        pl.semaphore_signal(turn, inc=1, device_id={"tm": partner}, device_id_type=mesh_id)
        on_both(lambda copy: copy.wait_send(), range(PIECES - 1, PIECES))

    @pl.when(core == 1)
    def _():
        pl.semaphore_wait(turn, 1)
        on_both(lambda copy: copy.start(), range(PIECES))
        on_both(lambda copy: copy.wait_send(), range(PIECES))

    for has, way, target in ((has_down, 0, below_ref), (has_up, 1, above_ref)):

        @pl.when(has)
        def _(way=way):
            for j in range(PIECES):
                piece(way, j).wait_recv()

        @pl.when(jnp.logical_not(has))
        def _(target=target):
            fill = pltpu.make_async_copy(zero, target, local_sems.at[0])
            fill.start()
            fill.wait()


def lead(field, rows, first, count, slabs):
    depth, _, plane = field.shape
    arrived = jax.ShapeDtypeStruct((2, rows, plane), jnp.float32)
    piece = jax.ShapeDtypeStruct((2, count, plane), jnp.float32)
    anywhere = pl.BlockSpec(memory_space=pl.ANY)
    return pl.pallas_call(
        functools.partial(lead_kernel, first, slabs),
        out_shape=(arrived, arrived, piece, piece),
        in_specs=[anywhere],
        out_specs=(anywhere,) * 4,
        scratch_shapes=[
            pltpu.VMEM((2, rows, plane), jnp.float32),
            pltpu.VMEM((depth, count, plane), jnp.float32),
            pltpu.SemaphoreType.DMA((2, PIECES)),
            pltpu.SemaphoreType.DMA((2, PIECES)),
            pltpu.SemaphoreType.DMA((3,)),
            pltpu.SemaphoreType.REGULAR,
        ],
        compiler_params=pltpu.CompilerParams(
            collective_id=0, has_side_effects=True, vmem_limit_bytes=58 * MIB
        ),
        name="lead",
    )(field)


def cut_kernel(field_ref, odd_ref, even_ref):
    up = field_ref.shape[0] - 2
    parity = odd_slab()
    odd_ref[...] = field_ref[pl.ds(parity * up, 2)]
    even_ref[...] = field_ref[pl.ds((1 - parity) * up, 2)]


def cut(field, first, count):
    depth, _, plane = field.shape
    piece = jax.ShapeDtypeStruct((2, count, plane), jnp.float32)
    block = pl.BlockSpec((2, 8, plane), lambda i: (0, i, 0))
    return pl.pallas_call(
        cut_kernel,
        out_shape=(piece, piece),
        grid=(count // 8,),
        in_specs=[pl.BlockSpec((depth, 8, plane), lambda i: (0, first // 8 + i, 0))],
        out_specs=(block, block),
        compiler_params=pltpu.CompilerParams(vmem_limit_bytes=46 * MIB),
        cost_estimate=pl.CostEstimate(
            flops=0, bytes_accessed=4 * count * plane * (depth + 4), transcendentals=0
        ),
        name="cut",
    )(field)


def project_kernel(projector_ref, field_ref, out_ref):
    high, low = parts(field_ref[0])
    out_ref[0] = product(projector_ref[...], high, low)


def block_sums(projector, field):
    depth, steps, plane = field.shape
    modes = projector.shape[0]
    return pl.pallas_call(
        project_kernel,
        out_shape=jax.ShapeDtypeStruct((depth, modes, plane), jnp.float32),
        grid=(depth, plane // TILE),
        in_specs=[
            pl.BlockSpec((modes, steps), lambda p, i: (0, 0)),
            pl.BlockSpec((1, steps, TILE), lambda p, i: (p, 0, i)),
        ],
        out_specs=pl.BlockSpec((1, modes, TILE), lambda p, i: (p, 0, i)),
        cost_estimate=pl.CostEstimate(
            flops=6 * modes * steps * depth * plane,
            bytes_accessed=4 * depth * plane * (steps + modes),
            transcendentals=0,
        ),
        compiler_params=pltpu.CompilerParams(vmem_limit_bytes=46 * MIB),
        name="block_sums",
    )(projector, field)


def stencil_bands():
    shape = (SPAN // EDGE, SPAN, EDGE)
    lane_out = lax.broadcasted_iota(jnp.int32, shape, 2)
    offset = lax.broadcasted_iota(jnp.int32, shape, 1) - EDGE - lane_out
    column = (lax.broadcasted_iota(jnp.int32, shape, 0) * EDGE + lane_out) % NY
    inside = (column + offset >= 0) & (column + offset < NY)
    size = jnp.abs(offset)
    near = (size == NY) | ((size == 1) & inside)
    far = (size == 2 * NY) | ((size == 2) & inside)
    return jnp.where(near, 16.0, jnp.where(far, -1.0, 0.0)).astype(jnp.bfloat16)


def local_kernel(
    table_ref,
    bands_ref,
    left_ref,
    mid_ref,
    right_ref,
    head_ref,
    carried_ref,
    absorb_ref,
    out_ref,
    high_ref,
    low_ref,
):
    depth, steps, width = mid_ref.shape
    spot, spots = pl.program_id(0), pl.num_programs(0)
    has_left = jnp.where(spot > 0, 1.0, 0.0)
    has_right = jnp.where(spot < spots - 1, 1.0, 0.0)
    factor = -DIFFUSION / 12.0
    table = table_ref[...]

    def put(p, rows, lanes, value):
        high, low = parts(value)
        high_ref[p, rows, lanes] = high
        low_ref[p, rows, lanes] = low

    own, ahead, later = slice(0, steps), slice(steps, steps + BAND), slice(steps + BAND, None)
    inner = slice(EDGE, EDGE + width)
    for p in range(depth):
        put(p, own, slice(0, EDGE), left_ref[p] * has_left)
        put(p, own, inner, mid_ref[p])
        put(p, own, slice(EDGE + width, None), right_ref[p] * has_right)
        put(p, ahead, inner, head_ref[p])
        put(p, later, inner, carried_ref[p])

    def one_span(g, _):
        base = pl.multiple_of(g * SPAN, SPAN)
        span = pl.ds(base, SPAN)
        inner_span = pl.ds(pl.multiple_of(base + EDGE, EDGE), SPAN)
        for p in range(depth):
            total = product(table, high_ref[p, :, inner_span], low_ref[p, :, inner_span])
            near, far = 0.0, 0.0
            for q in range(depth):
                if abs(q - p) == 1:
                    near = near + mid_ref[q, :, span]
                if abs(q - p) == 2:
                    far = far + mid_ref[q, :, span]
            scale = absorb_ref[pl.ds(p, 1), span] - 90.0 * factor
            out_ref[p, :, span] = (
                total + scale * mid_ref[p, :, span] + factor * (16.0 * near - far)
            )
        for k in range(SPAN // EDGE):
            window = pl.ds(pl.multiple_of(base + k * EDGE, EDGE), SPAN)
            tile = pl.ds(pl.multiple_of(base + k * EDGE, EDGE), EDGE)
            high = jnp.concatenate([high_ref[p, own, window] for p in range(depth)], axis=0)
            low = jnp.concatenate([low_ref[p, own, window] for p in range(depth)], axis=0)
            around = jnp.dot(high, bands_ref[k], preferred_element_type=jnp.float32)
            around = around + jnp.dot(low, bands_ref[k], preferred_element_type=jnp.float32)
            for p in range(depth):
                out_ref[p, :, tile] += factor * around[p * steps : (p + 1) * steps]
        return 0

    lax.fori_loop(0, width // SPAN, one_span, 0)


def local_part(table, bands, field, head, carried, absorption):
    depth, steps, plane = field.shape
    per = TILE // EDGE
    last = plane // EDGE - 1
    cols = table.shape[1]
    wide = (depth, cols, TILE + 2 * EDGE)
    return pl.pallas_call(
        local_kernel,
        out_shape=jax.ShapeDtypeStruct(field.shape, jnp.float32),
        grid=(plane // TILE,),
        in_specs=[
            pl.BlockSpec((steps, cols), lambda i: (0, 0)),
            pl.BlockSpec(bands.shape, lambda i: (0, 0, 0)),
            pl.BlockSpec((depth, steps, EDGE), lambda i: (0, 0, jnp.maximum(i * per - 1, 0))),
            pl.BlockSpec((depth, steps, TILE), lambda i: (0, 0, i)),
            pl.BlockSpec((depth, steps, EDGE), lambda i: (0, 0, jnp.minimum(i * per + per, last))),
            pl.BlockSpec((depth, BAND, TILE), lambda i: (0, 0, i)),
            pl.BlockSpec((depth, cols - steps - BAND, TILE), lambda i: (0, 0, i)),
            pl.BlockSpec((depth, TILE), lambda i: (0, i)),
        ],
        out_specs=pl.BlockSpec((depth, steps, TILE), lambda i: (0, 0, i)),
        scratch_shapes=[pltpu.VMEM(wide, jnp.bfloat16), pltpu.VMEM(wide, jnp.bfloat16)],
        compiler_params=pltpu.CompilerParams(vmem_limit_bytes=44 * MIB),
        cost_estimate=pl.CostEstimate(
            flops=6 * cols * steps * depth * plane,
            bytes_accessed=8 * depth * plane * steps,
            transcendentals=0,
        ),
        name="local_part",
    )(table, bands, field, field, field, head, carried, absorption)


def edge_terms(below, above, depth):
    factor = -DIFFUSION / 12.0
    ends = [None] * depth

    def add(p, value):
        if 0 <= p < depth:
            ends[p] = value if ends[p] is None else ends[p] + value

    add(0, 16.0 * below[1] - below[0])
    add(1, -below[1])
    add(depth - 1, 16.0 * above[0] - above[1])
    add(depth - 2, -above[0])
    return [0.0 if end is None else factor * end for end in ends]


def by_side(odd, even):
    lower = odd_slab() == 0
    below = [jnp.where(lower, odd[k], even[k]) for k in range(2)]
    above = [jnp.where(lower, even[k], odd[k]) for k in range(2)]
    return below, above


def edge_kernel(sided, image_ref, one_ref, other_ref, out_ref):
    depth = image_ref.shape[0]
    below, above = (one_ref, other_ref) if sided else by_side(one_ref, other_ref)
    terms = edge_terms(below, above, depth)
    for p in range(depth):
        out_ref[p] = image_ref[p] + terms[p]


def hold_kernel(first, image_ref, out_ref, sem):
    rows = out_ref.shape[1]
    copy = pltpu.make_async_copy(image_ref.at[:, pl.ds(first, rows)], out_ref, sem)
    copy.start()
    copy.wait()


def hold_rows(image, first, rows):
    depth, _, plane = image.shape
    return pl.pallas_call(
        functools.partial(hold_kernel, first),
        out_shape=jax.ShapeDtypeStruct((depth, rows, plane), jnp.float32),
        in_specs=[pl.BlockSpec(memory_space=pl.ANY)],
        out_specs=pl.BlockSpec(memory_space=pltpu.VMEM),
        scratch_shapes=[pltpu.SemaphoreType.DMA(())],
        compiler_params=pltpu.CompilerParams(vmem_limit_bytes=44 * MIB),
        name="hold_rows",
    )(image)


def last_kernel(first, width, image_ref, held_ref, odd_ref, even_ref, out_ref, done, sems):
    depth, rows, plane = held_ref.shape
    stores = []
    for j in range(plane // width):
        lanes = pl.ds(j * width, width)
        below, above = by_side(odd_ref[:, :, lanes], even_ref[:, :, lanes])
        terms = edge_terms(below, above, depth)
        for p in range(depth):
            done[p, :, lanes] = held_ref[p, :, lanes] + terms[p]
        store = pltpu.make_async_copy(
            done.at[:, :, lanes], out_ref.at[:, pl.ds(first, rows), lanes], sems.at[j]
        )
        store.start()
        stores.append(store)
    for store in stores:
        store.wait()


def add_last(image, held, odd, even, first):
    depth, rows, plane = held.shape
    width = TILE
    anywhere = pl.BlockSpec(memory_space=pl.ANY)
    vmem = pl.BlockSpec(memory_space=pltpu.VMEM)
    return pl.pallas_call(
        functools.partial(last_kernel, first, width),
        out_shape=jax.ShapeDtypeStruct(image.shape, jnp.float32),
        in_specs=[anywhere, vmem, vmem, vmem],
        out_specs=anywhere,
        scratch_shapes=[
            pltpu.VMEM((depth, rows, plane), jnp.float32),
            pltpu.SemaphoreType.DMA((plane // width,)),
        ],
        input_output_aliases={0: 0},
        compiler_params=pltpu.CompilerParams(vmem_limit_bytes=8 * MIB),
        name="add_last",
    )(image, held, odd, even)


def add_edges(image, one, other, first, rows, width, sided=False):
    depth, _, plane = image.shape
    count = one.shape[1]
    at = first // rows
    return pl.pallas_call(
        functools.partial(edge_kernel, sided),
        out_shape=jax.ShapeDtypeStruct(image.shape, jnp.float32),
        grid=(count // rows, plane // width),
        in_specs=[
            pl.BlockSpec((depth, rows, width), lambda i, j: (0, at + i, j)),
            pl.BlockSpec((2, rows, width), lambda i, j: (0, i, j)),
            pl.BlockSpec((2, rows, width), lambda i, j: (0, i, j)),
        ],
        out_specs=pl.BlockSpec((depth, rows, width), lambda i, j: (0, at + i, j)),
        input_output_aliases={0: 0},
        cost_estimate=pl.CostEstimate(
            flops=8 * depth * count * plane,
            bytes_accessed=4 * count * plane * (2 * depth + 4),
            transcendentals=0,
        ),
        compiler_params=pltpu.CompilerParams(vmem_limit_bytes=16 * MIB),
        name="add_edges",
    )(image, one, other)


def per_device(adjoint_field, absorption, mode_rates, mode_weights):
    steps, _, plane = adjoint_field.shape
    groups = lax.axis_size("tm")
    slabs = lax.axis_size("space")
    field = jnp.transpose(adjoint_field, (1, 0, 2))

    def both_ways(lowest):
        pairs = [(i, i + 1) for i in range(lowest, slabs - 1, 2)]
        return pairs + [(j, i) for i, j in pairs]

    starts = [sum(CHUNKS[:k]) for k in range(len(CHUNKS))]
    below, above, over_odd, over_even = lead(field, CHUNKS[0], CHUNKS[0], CHUNKS[1], slabs)
    odds, evens = [], []
    source = field
    for k, count in enumerate(CHUNKS[1:], 1):
        if k > 1:
            over_odd, over_even = cut(source, starts[k], count)
        odds.append(lax.ppermute(over_odd, "space", both_ways(1)))
        evens.append(lax.ppermute(over_even, "space", both_ways(0)))
        source, _, _ = lax.optimization_barrier((source, over_odd, over_even))
        if k == 1:
            early = source

    scaled = mode_rates / (steps * groups)
    mode_gain = mode_weights * jnp.sqrt(-jnp.expm1(-2.0 * scaled))
    table, projector = history_tables(scaled, mode_gain, steps)

    mine_first = early[:, :BAND]
    head = lax.ppermute(mine_first, "tm", [(g + 1, g) for g in range(groups - 1)])
    sums = block_sums(projector, early)
    decay = jnp.exp(-scaled * steps)[None, :, None]
    swap = [(g, g + 1 - 2 * (g % 2)) for g in range(groups)]
    other = lax.ppermute(sums, "tm", swap)
    core = lax.axis_index("tm") % 2
    half = plane // 2
    mine_half = lax.dynamic_slice_in_dim(sums, core * half, half, axis=2)
    other_half = lax.dynamic_slice_in_dim(other, core * half, half, axis=2)
    pair_half = jnp.where(
        core == 0, mine_half + decay * other_half, other_half + decay * mine_half
    )
    later = None
    for _ in range(groups // 2 - 1):
        sent = pair_half if later is None else pair_half + decay * decay * later
        later = lax.ppermute(sent, "tm", [(g + 2, g) for g in range(groups - 2)])
    later_other = lax.ppermute(later, "tm", swap)
    later_full = jnp.where(
        core == 0,
        jnp.concatenate([later, later_other], axis=2),
        jnp.concatenate([later_other, later], axis=2),
    )
    carried = jnp.where(core == 0, other + decay * later_full, later_full)

    image = local_part(table, stencil_bands(), field, head, carried, absorption)
    held = hold_rows(image, starts[-1], CHUNKS[-1])
    image = add_edges(image, below, above, 0, 8, plane, sided=True)
    for k in range(1, len(CHUNKS) - 1):
        image = add_edges(image, odds[k - 1], evens[k - 1], starts[k], 8, plane)
    image = add_last(image, held, odds[-1], evens[-1], starts[-1])
    return jnp.transpose(image, (1, 0, 2))


def solution(mesh):
    return jax.shard_map(
        per_device,
        mesh=mesh,
        in_specs=(P("tm", "space", None), P("space", None), P(), P()),
        out_specs=P("tm", "space", None),
        check_vma=False,
    )
```
